32 devices in a mesh: field: 2 (over y), sky: 4 (over z), epoch: 2 (over x), vel: 2 (over core).
Axes of the slice: x: 2, y: 2, z: 4, core: 2. Of those that a mesh axis runs over, the one named last changes fastest.
Arguments:
- images: bfloat16 [64, 8, 128, 128], P(('epoch', 'vel'), ('field', 'sky')), parts along dimension 1, may hold values from -6 to 6
- variances: bfloat16 [64, 8, 128, 128], P(('epoch', 'vel'), ('field', 'sky')), parts along dimension 1, may hold values from 0.5 to 2
- valid: int32 [64, 8], P(('epoch', 'vel'), ('field', 'sky')), parts along dimension 1, may hold values from 0 to 1, as said below
- psf_sigma: float32 [128], P(('field', 'epoch', 'vel')), parts along dimension 0, may hold values from 0.8 to 2.5
- offsets: int32 [2, 16, 64], P(None, None, 'epoch'), may hold values from -12 to 12, as said below
Outputs:
- likelihood: float32 [16, 8, 128, 128], P(('epoch', 'vel'), ('field', 'sky')), parts along dimension 1
- flux: float32 [16, 8, 128, 128], P(('epoch', 'vel'), ('field', 'sky')), parts along dimension 1
The draws below stay inside these ranges and needn't reach their ends.
There are 2 independent parts, one for each index of `field`. The reference program is written for one: setup_inputs(seed, part) draws one part's arguments, and reference() takes and returns one part's arrays. A program takes and returns all parts, laid end to end along the dimension named above; an argument that names none is the same for every part. Nothing has to cross between parts.
Inputs may be any that keep to these rules, and one draw needn't show every extreme that they name: Each hypothesis moves linearly: offsets[c, k, e] = floor(s[c, k] * e / 63) for integer speeds s within the range; both ends of the range are reached. `valid`: in one tile of the field, drawn from the seed, exactly one epoch is usable; in every other tile each frame is usable with probability 3/4, independently.
All inputs are finite; a program needn't handle non-finite values.
Results may differ from the reference program's by a relative error of at most 0.0058.
Values may be sent and summed in bfloat16 or wider, within the bound.
A program may use at most 64 MiB of HBM per device.

```python
import math
import jax
import jax.numpy as jnp
from jax import lax

TILE = 128
VELS = 16
REACH = 12
PSFR = 7
GRID_X = 4
EPOCHS = 64
N_SKY = 4


def draw_offsets(key, part):
    speeds = jax.random.randint(key, (2, VELS), -REACH, REACH + 1).astype(jnp.int32)
    speeds = speeds.at[1, 0].set(REACH).at[0, 1].set(-REACH)
    epoch_ids = jnp.arange(EPOCHS, dtype=jnp.int32)
    return (speeds[:, :, None] * epoch_ids[None, None, :] // (EPOCHS - 1)).astype(jnp.int32)


def draw_valid(key, part):
    levels = jax.random.randint(jax.random.fold_in(key, 11), (EPOCHS, N_SKY), 0, 4)
    usable = (levels < 3).astype(jnp.int32)
    sparse_tile = jax.random.randint(jax.random.fold_in(key, 12), (), 0, N_SKY)
    kept_epoch = jax.random.randint(jax.random.fold_in(key, 13), (), 0, EPOCHS)
    tile_ids = jnp.arange(N_SKY, dtype=jnp.int32)
    epoch_ids = jnp.arange(EPOCHS, dtype=jnp.int32)
    single = (epoch_ids[:, None] == kept_epoch).astype(jnp.int32) * jnp.ones((1, N_SKY), jnp.int32)
    return jnp.where(tile_ids[None, :] == sparse_tile, single, usable).astype(jnp.int32)


def shard_levels(own_key, shape, split, least, top_value):
    def one(axis_at, blocks):
        draws = jax.random.uniform(jax.random.fold_in(jax.random.fold_in(own_key, 6), axis_at), (blocks,), jnp.float32, least / len(split), top_value / len(split))
        return jnp.repeat(jnp.exp(draws), shape[axis_at] // blocks).reshape((-1,) + (1,) * (len(shape) - axis_at - 1))

    loudness = one(*split[0])
    for cut in split[1:]:
        loudness = loudness * one(*cut)
    return loudness


def scatter_about(stream_key, dims, scale, reach, shards=(), held_as=jnp.bfloat16):
    array = scale * jax.random.normal(stream_key, dims, jnp.float32)
    if shards:
        array = array * shard_levels(stream_key, dims, shards, -0.22, 0.18)
    return jnp.clip(array, -reach, reach).astype(held_as)


def setup_inputs(seed: int = 0, part: int = 0) -> dict:
    streams_of = jax.random.split(jax.random.key(seed), 6)
    own_keys = jax.random.split(jax.random.fold_in(streams_of[5], part), 6)
    images = scatter_about(own_keys[0], (EPOCHS, N_SKY, TILE, TILE), 1.0, 6.0, ((0, 4), (1, 4)))
    variances = jnp.clip(jnp.exp(math.log(2.0) - 1.3862944 * jax.random.uniform(own_keys[1], (EPOCHS, N_SKY, TILE, TILE), jnp.float32) ** shard_levels(own_keys[1], (EPOCHS, N_SKY, TILE, TILE), ((0, 4), (1, 4)), -0.2, 0.2)), 0.5, 2.0).astype(jnp.bfloat16)
    valid = draw_valid(jax.random.fold_in(jax.random.fold_in(streams_of[5], part), 71), part)
    psf_sigma = jnp.clip(jnp.exp(math.log(2.5) - 1.13943427 * jax.random.uniform(own_keys[3], (EPOCHS,), jnp.float32) ** shard_levels(own_keys[3], (EPOCHS,), ((0, 4),), -0.2, 0.2)), 0.8, 2.5)
    offsets = draw_offsets(jax.random.fold_in(streams_of[5], 71), part)
    return dict(images=images, variances=variances, valid=valid, psf_sigma=psf_sigma, offsets=offsets)


phi_floor = 0.25

def round_keep(values):
    rounded = values.astype(jnp.bfloat16)
    rounded = lax.optimization_barrier(rounded)
    return rounded.astype(jnp.float32)

def kernel_taps(psf_sigma):
    spread = jnp.arange(-PSFR, PSFR + 1).astype(jnp.float32)
    profile = jnp.exp(-0.5 * (spread[None, :] / psf_sigma[:, None]) ** 2)
    profile = profile / lax.optimization_barrier(jnp.sum(profile, axis=1, keepdims=True))
    return (round_keep(profile), round_keep(profile * profile))

def whole_field(tiles):
    epoch_count = tiles.shape[0]
    grid_rows = N_SKY // GRID_X
    placed = jnp.roll(tiles, GRID_X // 2, axis=1)
    shaped = placed.reshape(epoch_count, grid_rows, GRID_X, TILE, TILE)
    return shaped.transpose(0, 1, 3, 2, 4).reshape(epoch_count, grid_rows * TILE, GRID_X * TILE)

def back_to_tiles(field):
    leading = field.shape[0]
    grid_rows = N_SKY // GRID_X
    shaped = field.reshape(leading, grid_rows, TILE, GRID_X, TILE)
    placed = shaped.transpose(0, 1, 3, 2, 4).reshape(leading, N_SKY, TILE, TILE)
    return jnp.roll(placed, -(GRID_X // 2), axis=1)

def correlate(field, kernel, axis):
    widths = [(0, 0), (0, 0), (0, 0)]
    widths[axis] = (PSFR, PSFR)
    padded = jnp.pad(field, widths)
    length = field.shape[axis]
    summed = jnp.zeros(field.shape, jnp.float32)
    for tap_index in range(2 * PSFR + 1):
        window = lax.slice_in_dim(padded, tap_index, tap_index + length, axis=axis)
        summed = summed + kernel[:, tap_index][:, None, None] * window
    return summed

def reference(images, variances, valid, psf_sigma, offsets):
    usable = valid.astype(jnp.float32)[:, :, None, None]
    scaled = images.astype(jnp.float32) / variances.astype(jnp.float32) * usable
    inverse = usable / variances.astype(jnp.float32)
    scaled = whole_field(round_keep(scaled))
    inverse = whole_field(round_keep(inverse))
    edges = ((0, 0), (REACH, REACH), (REACH, REACH))
    scaled = jnp.pad(scaled, edges)
    inverse = jnp.pad(inverse, edges)
    first_taps, second_taps = kernel_taps(psf_sigma)
    psi = correlate(round_keep(correlate(scaled, first_taps, 1)), first_taps, 2)
    phi = correlate(round_keep(correlate(inverse, second_taps, 1)), second_taps, 2)
    paired = jnp.stack([psi, phi], axis=1)
    height = paired.shape[2] - 2 * REACH
    breadth = paired.shape[3] - 2 * REACH

    def stack_one(motion):

        def accumulate(epoch_id, summed):
            epoch_map = lax.dynamic_index_in_dim(paired, epoch_id, 0, keepdims=False)
            start_y = (REACH + motion[0, epoch_id]).astype(jnp.int32)
            start_x = (REACH + motion[1, epoch_id]).astype(jnp.int32)
            window = lax.dynamic_slice(epoch_map, (jnp.zeros((), jnp.int32), start_y, start_x), (2, height, breadth))
            return summed + window
        return lax.fori_loop(0, EPOCHS, accumulate, jnp.zeros((2, height, breadth), jnp.float32))
    sums = lax.map(stack_one, jnp.transpose(offsets, (1, 0, 2)))
    psi_sum = sums[:, 0]
    phi_sum = jnp.maximum(sums[:, 1], phi_floor)
    likelihood = psi_sum / jnp.sqrt(phi_sum)
    flux = psi_sum / phi_sum
    return (back_to_tiles(likelihood), back_to_tiles(flux))
```

```python
import functools

import jax
import jax.numpy as jnp
from jax import lax
from jax.experimental import pallas as pl
from jax.experimental.pallas import tpu as pltpu
from jax.sharding import PartitionSpec as P

VELS = 16
REACH = 12
PSFR = 7
GRID_X = 4
MARGIN = REACH + PSFR
LANES = 128

phi_floor = 0.25


def shifted(block, axis, distance):
    devices = range(lax.axis_size(axis))
    route = [((i - distance) % len(devices), i) for i in devices]
    return lax.ppermute(block, axis, route)


def positions(index, tile):
    return jnp.where(
        index < tile,
        index,
        jnp.where(
            index < tile + MARGIN,
            index - tile - MARGIN,
            jnp.where(index < tile + 2 * MARGIN, index - MARGIN, 4 * tile),
        ),
    )


def band(held, out, sigma, scale, tile):
    distance = positions(held, tile) - (out - REACH)
    away = distance.astype(jnp.float32) / sigma
    profile = jnp.exp(-0.5 * away * away) * scale
    profile = jnp.where(jnp.abs(distance) <= PSFR, profile, 0.0)
    return profile.astype(jnp.bfloat16), (profile * profile).astype(jnp.bfloat16)


def stack_kernel(tile, offsets, sigmas, order, first, own, halo, out, plane_a, plane_b):
    epochs, maps, rows_in, _ = own.shape
    rows_out = plane_a.shape[1]
    width = 2 * LANES

    def correlate(e, carry):
        sigma = jnp.full((8, LANES), sigmas[e], jnp.float32)
        tap = lax.broadcasted_iota(jnp.int32, (8, LANES), 1) - PSFR
        spread = tap.astype(jnp.float32) / sigma
        norm = jnp.sum(
            jnp.where(jnp.abs(tap) <= PSFR, jnp.exp(-0.5 * spread * spread), 0.0),
            axis=1,
            keepdims=True,
        )
        scale = (1.0 / norm)[:1]
        sig = sigma[:1, :1]
        shape = (rows_out, rows_in)
        row_bands = band(
            lax.broadcasted_iota(jnp.int32, shape, 1),
            lax.broadcasted_iota(jnp.int32, shape, 0),
            sig, scale, tile,
        )
        shape = (width, width)
        col_bands = band(
            lax.broadcasted_iota(jnp.int32, shape, 0),
            lax.broadcasted_iota(jnp.int32, shape, 1),
            sig, scale, tile,
        )
        for m in range(maps):
            held = jnp.concatenate([own[e, m], halo[e, m]], axis=1)
            rows = jnp.dot(row_bands[m], held, preferred_element_type=jnp.float32)
            done = jnp.dot(
                rows.astype(jnp.bfloat16), col_bands[m], preferred_element_type=jnp.float32
            )
            plane_a[maps * e + m] = done[:, :LANES]
            plane_b[maps * e + m] = done[:, LANES:]
        return carry

    lax.fori_loop(0, epochs, correlate, 0)
    lane = lax.broadcasted_iota(jnp.int32, (tile, LANES), 1)

    def stack(slot, carry):
        k = order[slot]
        summed = [jnp.zeros((tile, LANES), jnp.float32) for _ in range(maps)]
        for e in range(epochs):
            down = offsets[0, k, first[0] + e] + REACH
            right = offsets[1, k, first[0] + e] + REACH
            for m in range(maps):
                left_part = plane_a[maps * e + m, pl.ds(down, tile), :]
                right_part = plane_b[maps * e + m, pl.ds(down, tile), :]
                merged = jnp.where(lane >= right, left_part, right_part)
                summed[m] += pltpu.roll(merged, LANES - right, axis=1)
        for m in range(maps):
            out[slot, m] = summed[m].astype(jnp.bfloat16)
        return carry

    lax.fori_loop(0, out.shape[0], stack, 0)


def on_device(images, variances, valid, psf_sigma, offsets):
    epochs = images.shape[0]
    tile = images.shape[-1]
    usable = valid[:, 0].astype(jnp.float32)[:, None, None]
    scaled = images[:, 0].astype(jnp.float32) / variances[:, 0].astype(jnp.float32) * usable
    inverse = usable / variances[:, 0].astype(jnp.float32)
    own = jnp.stack([scaled.astype(jnp.bfloat16), inverse.astype(jnp.bfloat16)], axis=1)
    tile_count = lax.axis_size("sky")
    position = (lax.axis_index("sky") + GRID_X // 2) % tile_count
    column = position % GRID_X
    left = shifted(own[..., tile - MARGIN :], "sky", 1)
    right = shifted(own[..., :MARGIN], "sky", -1)
    left = jnp.where(column > 0, left, jnp.zeros_like(left))
    right = jnp.where(column < GRID_X - 1, right, jnp.zeros_like(right))
    blank = jnp.zeros(own.shape[:3] + (LANES - 2 * MARGIN,), jnp.bfloat16)
    halo = jnp.concatenate([left, right, blank], axis=3)
    if tile_count > GRID_X:
        both = jnp.concatenate([own, halo], axis=3)
        upper = shifted(both[:, :, tile - MARGIN :], "sky", GRID_X)
        lower = shifted(both[:, :, :MARGIN], "sky", -GRID_X)
        upper = jnp.where(position >= GRID_X, upper, jnp.zeros_like(upper))
        lower = jnp.where(position < tile_count - GRID_X, lower, jnp.zeros_like(lower))
        blank = jnp.zeros(both.shape[:2] + (LANES - 2 * MARGIN, both.shape[3]), jnp.bfloat16)
        both = jnp.concatenate([both, upper, lower, blank], axis=2)
        own, halo = both[..., :tile], both[..., tile:]
    pairs = lax.axis_size("vel")
    blocks = lax.axis_size("epoch")
    member = lax.axis_index("vel")
    group = lax.axis_index("epoch")
    block = VELS // (blocks * pairs)
    slot = jnp.arange(VELS, dtype=jnp.int32)
    to_member = (member + slot // (blocks * block)) % pairs
    to_group = (group + slot // block % blocks) % blocks
    order = (to_group * pairs + to_member) * block + slot % block
    first = (member * epochs).astype(jnp.int32)[None]
    rows_out = -(-(tile + 2 * REACH) // 16) * 16
    smem = pl.BlockSpec(memory_space=pltpu.SMEM)
    vmem = pl.BlockSpec(memory_space=pltpu.VMEM)
    partial = pl.pallas_call(
        functools.partial(stack_kernel, tile),
        out_shape=jax.ShapeDtypeStruct((VELS, 2, tile, tile), jnp.bfloat16),
        in_specs=[smem, smem, smem, smem, vmem, vmem],
        out_specs=vmem,
        scratch_shapes=[
            pltpu.VMEM((2 * epochs, rows_out, LANES), jnp.float32),
            pltpu.VMEM((2 * epochs, rows_out, LANES), jnp.float32),
        ],
        compiler_params=pltpu.CompilerParams(vmem_limit_bytes=48 * 2**20),
    )(offsets, psf_sigma, order.astype(jnp.int32), first, own, halo)
    half = blocks * block
    sums = partial[:half].astype(jnp.float32)
    for away in range(1, pairs):
        came = shifted(partial[away * half : (away + 1) * half], "vel", away)
        sums = sums + came.astype(jnp.float32)
    total = sums[:block]
    for away in range(1, blocks):
        sent = sums[away * block : (away + 1) * block].astype(jnp.bfloat16)
        total = total + shifted(sent, "epoch", away).astype(jnp.float32)
    psi_sum = total[:, 0]
    phi_sum = jnp.maximum(total[:, 1], phi_floor)
    likelihood = psi_sum / jnp.sqrt(phi_sum)
    flux = psi_sum / phi_sum
    return (likelihood[:, None], flux[:, None])


def solution(mesh):
    placed = (
        P(("epoch", "vel"), ("field", "sky"), None, None),
        P(("epoch", "vel"), ("field", "sky"), None, None),
        P(("epoch", "vel"), ("field", "sky")),
        P(("field", "epoch", "vel")),
        P(None, None, "epoch"),
    )
    return jax.shard_map(
        on_device,
        mesh=mesh,
        in_specs=placed,
        out_specs=(
            P(("epoch", "vel"), ("field", "sky"), None, None),
            P(("epoch", "vel"), ("field", "sky"), None, None),
        ),
        check_vma=False,
    )
```

```python
import functools

import jax
import jax.numpy as jnp
from jax import lax
from jax.experimental import pallas as pl
from jax.experimental.pallas import tpu as pltpu
from jax.sharding import PartitionSpec as P

VELS = 16
REACH = 12
PSFR = 7
GRID_X = 4
MARGIN = REACH + PSFR
LANES = 128

phi_floor = 0.25


def shifted(block, axis, distance):
    devices = range(lax.axis_size(axis))
    route = [((i - distance) % len(devices), i) for i in devices]
    return lax.ppermute(block, axis, route)


def positions(index, tile):
    return jnp.where(
        index < tile,
        index,
        jnp.where(
            index < tile + MARGIN,
            index - tile - MARGIN,
            jnp.where(index < tile + 2 * MARGIN, index - MARGIN, 4 * tile),
        ),
    )


FAR = -1.0e9


def exponents(distance):
    away = distance.astype(jnp.float32)
    return jnp.where(jnp.abs(distance) <= PSFR, -0.5 * away * away, FAR)


def fused_kernel(plan, *refs):
    tile, sky, blocks, block, epochs, exchange = plan
    if exchange:
        (offsets, sigmas, valid, images, variances, likelihood, flux, plane_a, plane_b, row_q,
         own_q, side_q, bands, send_v, recv_v, send_x, recv_x, keep, sv, rv, sx, rx,
         own, building, sent_sides, came_sides, sz, rz) = refs
    else:
        (offsets, sigmas, own, halo, likelihood, flux, plane_a, plane_b, row_q,
         own_q, side_q, bands, send_v, recv_v, send_x, recv_x, keep, sv, rv, sx, rx) = refs
    maps = 2
    slots = LANES // MARGIN
    rows_in = row_q.shape[1]
    rows_out = plane_a.shape[1]
    width = 2 * LANES
    mesh_id = pl.DeviceIdType.MESH
    me = lax.axis_index("sky")
    group = lax.axis_index("epoch")
    member = lax.axis_index("vel")
    column = lax.rem(lax.rem(me + GRID_X // 2, sky), GRID_X)
    before = lax.rem(me + sky - 1, sky)
    after = lax.rem(me + 1, sky)
    partner = 1 - member

    barrier = pltpu.get_barrier_semaphore()
    greeted = 1
    pl.semaphore_signal(barrier, inc=1, device_id={"vel": partner}, device_id_type=mesh_id)
    for a in range(1, blocks):
        peer = lax.rem(group + a, blocks)
        pl.semaphore_signal(barrier, inc=1, device_id={"epoch": peer}, device_id_type=mesh_id)
        greeted += 1
    if exchange:
        for other in (before, after):
            pl.semaphore_signal(barrier, inc=1, device_id={"sky": other}, device_id_type=mesh_id)
            greeted += 1

    if exchange:
        groups = sent_sides.shape[1]
        lane = lax.broadcasted_iota(jnp.int32, (tile, LANES), 1)

        def side_copy(to_after, g):
            return pltpu.make_async_remote_copy(
                src_ref=sent_sides.at[to_after, g],
                dst_ref=came_sides.at[to_after, g],
                send_sem=sz.at[to_after, g],
                recv_sem=rz.at[to_after, g],
                device_id={"sky": after if to_after else before},
                device_id_type=mesh_id,
            )

        building[...] = jnp.zeros_like(building)

        @pl.when(column == 0)
        def _():
            came_sides[1] = jnp.zeros_like(came_sides[1])

        @pl.when(column == GRID_X - 1)
        def _():
            came_sides[0] = jnp.zeros_like(came_sides[0])

        pl.semaphore_wait(barrier, greeted)

        def weigh(e, carry):
            s = lax.rem(e, slots)
            g = e // slots
            usable = valid[e, 0].astype(jnp.float32)
            inverse = usable / variances[e, 0].astype(jnp.float32)
            scaled = images[e, 0].astype(jnp.float32) * inverse
            to_slot = MARGIN * s
            to_mirror = MARGIN * (slots - 1 - s)
            for m, field in enumerate((scaled, inverse)):
                own[e, m] = field.astype(jnp.bfloat16)
                low = pltpu.roll(field, to_mirror, axis=1)
                high = pltpu.roll(field, to_slot + MARGIN, axis=1)
                at_low = (lane >= to_mirror) & (lane < to_mirror + MARGIN)
                at_high = (lane >= to_slot) & (lane < to_slot + MARGIN)
                building[0, m] = jnp.where(at_low, low, building[0, m])
                building[1, m] = jnp.where(at_high, high, building[1, m])

            @pl.when((s == slots - 1) | (e == epochs - 1))
            def _():
                sent_sides[0, g] = building[0].astype(jnp.bfloat16)
                sent_sides[1, g] = building[1].astype(jnp.bfloat16)

                @pl.when(column > 0)
                def _():
                    side_copy(0, g).start()

                @pl.when(column < GRID_X - 1)
                def _():
                    side_copy(1, g).start()

            return carry

        lax.fori_loop(0, epochs, weigh, 0)
    else:
        pl.semaphore_wait(barrier, greeted)

    shape = (rows_out, rows_in)
    row_q[...] = exponents(
        positions(lax.broadcasted_iota(jnp.int32, shape, 1), tile)
        - lax.broadcasted_iota(jnp.int32, shape, 0) + REACH
    )
    shape = (LANES, width)
    held = lax.broadcasted_iota(jnp.int32, shape, 0)
    shifted_out = lax.broadcasted_iota(jnp.int32, shape, 1) - REACH
    own_q[...] = exponents(held - shifted_out)
    if exchange:
        for s in range(slots):
            low, high = MARGIN * s, MARGIN * (slots - 1 - s)
            pixel = jnp.where(
                (held >= low) & (held < low + MARGIN),
                held - low - MARGIN,
                jnp.where((held >= high) & (held < high + MARGIN), held - high + tile, 4 * tile),
            )
            side_q[s] = exponents(pixel - shifted_out)
    else:
        side_q[0] = exponents(positions(held + tile, tile) - shifted_out)

    def correlate(e, carry):
        sigma = jnp.full((8, LANES), sigmas[e], jnp.float32)
        power = 1.0 / (sigma * sigma)
        tap = lax.broadcasted_iota(jnp.int32, (8, LANES), 1) - PSFR
        norm = jnp.sum(jnp.exp(exponents(tap) * power), axis=1, keepdims=True)
        scale = (1.0 / norm)[:1]
        power = power[:1, :1]

        def both(q):
            profile = jnp.exp(q * power) * scale
            return profile.astype(jnp.bfloat16), (profile * profile).astype(jnp.bfloat16)

        row_bands = both(row_q[...])
        s = lax.rem(e, slots) if exchange else 0
        for part, q in enumerate((own_q[...], side_q[s])):
            for m, made in enumerate(both(q)):
                bands[m, part * LANES : (part + 1) * LANES] = made
        if exchange:
            g = e // slots

            @pl.when(s == 0)
            def _():
                @pl.when(column < GRID_X - 1)
                def _():
                    side_copy(0, g).wait_recv()

                @pl.when(column > 0)
                def _():
                    side_copy(1, g).wait_recv()

            lane = lax.broadcasted_iota(jnp.int32, (tile, LANES), 1)
            in_slot = (lane >= MARGIN * s) & (lane < MARGIN * s + MARGIN)
        for m in range(maps):
            if exchange:
                side = jnp.where(
                    in_slot,
                    came_sides[1, g, m].astype(jnp.float32),
                    came_sides[0, g, m].astype(jnp.float32),
                ).astype(jnp.bfloat16)
            else:
                side = halo[e, m]
            held = jnp.concatenate([own[e, m], side], axis=1)
            rows = jnp.dot(row_bands[m], held, preferred_element_type=jnp.float32)
            done = jnp.dot(
                rows.astype(jnp.bfloat16), bands[m], preferred_element_type=jnp.float32
            )
            plane_a[maps * e + m] = done[:, :LANES]
            plane_b[maps * e + m] = done[:, LANES:]
        return carry

    lax.fori_loop(0, epochs, correlate, 0)

    def vel_copy(at):
        return pltpu.make_async_remote_copy(
            src_ref=send_v.at[at], dst_ref=recv_v.at[at], send_sem=sv.at[at], recv_sem=rv.at[at],
            device_id={"vel": partner}, device_id_type=mesh_id,
        )

    def epoch_copy(at):
        peer = lax.rem(group + 1 + at // block, blocks)
        return pltpu.make_async_remote_copy(
            src_ref=send_x.at[at], dst_ref=recv_x.at[at], send_sem=sx.at[at], recv_sem=rx.at[at],
            device_id={"epoch": peer}, device_id_type=mesh_id,
        )

    first = member * epochs

    def stack(slot, carry):
        a = blocks - 1 - slot // (2 * block)
        b = 1 - lax.rem(slot // block, 2)
        j = lax.rem(slot, block)
        at = a * block + j
        k = (lax.rem(group + a, blocks) * 2 + lax.rem(member + b, 2)) * block + j
        lane = lax.broadcasted_iota(jnp.int32, (tile, LANES), 1)
        summed = [jnp.zeros((tile, LANES), jnp.float32) for _ in range(maps)]
        for e in range(epochs):
            down = offsets[0, k, first + e] + REACH
            right = offsets[1, k, first + e] + REACH
            for m in range(maps):
                left_part = plane_a[maps * e + m, pl.ds(down, tile), :]
                right_part = plane_b[maps * e + m, pl.ds(down, tile), :]
                merged = jnp.where(lane >= right, left_part, right_part)
                summed[m] += pltpu.roll(merged, LANES - right, axis=1)
        for m in range(maps):
            keep[j, m] = summed[m]

        @pl.when(b == 1)
        def _():
            send_v[at] = keep[j].astype(jnp.bfloat16)
            vel_copy(at).start()

        @pl.when(b == 0)
        def _():
            vel_copy(at).wait_recv()
            keep[j] = keep[j] + recv_v[at].astype(jnp.float32)

            @pl.when(a > 0)
            def _():
                send_x[at - block] = keep[j].astype(jnp.bfloat16)
                epoch_copy(at - block).start()

        return carry

    lax.fori_loop(0, 2 * blocks * block, stack, 0)

    def finish(j, carry):
        total = keep[j]
        for a in range(1, blocks):
            at = (a - 1) * block + j
            epoch_copy(at).wait_recv()
            total = total + recv_x[at].astype(jnp.float32)
        phi = jnp.maximum(total[1], phi_floor)
        likelihood[j, 0] = total[0] / jnp.sqrt(phi)
        flux[j, 0] = total[0] / phi
        return carry

    lax.fori_loop(0, block, finish, 0)

    def drain_v(at, carry):
        vel_copy(at).wait_send()
        return carry

    lax.fori_loop(0, blocks * block, drain_v, 0)

    def drain_x(at, carry):
        epoch_copy(at).wait_send()
        return carry

    lax.fori_loop(0, (blocks - 1) * block, drain_x, 0)
    if exchange:

        def drain_z(g, carry):
            @pl.when(column > 0)
            def _():
                side_copy(0, g).wait_send()

            @pl.when(column < GRID_X - 1)
            def _():
                side_copy(1, g).wait_send()

            return carry

        lax.fori_loop(0, groups, drain_z, 0)


def strips(own, tile_count, tile):
    position = (lax.axis_index("sky") + GRID_X // 2) % tile_count
    column = position % GRID_X
    left = shifted(own[..., tile - MARGIN :], "sky", 1)
    right = shifted(own[..., :MARGIN], "sky", -1)
    left = jnp.where(column > 0, left, jnp.zeros_like(left))
    right = jnp.where(column < GRID_X - 1, right, jnp.zeros_like(right))
    blank = jnp.zeros(own.shape[:3] + (LANES - 2 * MARGIN,), jnp.bfloat16)
    both = jnp.concatenate([own, left, right, blank], axis=3)
    upper = shifted(both[:, :, tile - MARGIN :], "sky", GRID_X)
    lower = shifted(both[:, :, :MARGIN], "sky", -GRID_X)
    upper = jnp.where(position >= GRID_X, upper, jnp.zeros_like(upper))
    lower = jnp.where(position < tile_count - GRID_X, lower, jnp.zeros_like(lower))
    blank = jnp.zeros(both.shape[:2] + (LANES - 2 * MARGIN, both.shape[3]), jnp.bfloat16)
    both = jnp.concatenate([both, upper, lower, blank], axis=2)
    return both[..., :tile], both[..., tile:]


def on_device(images, variances, valid, psf_sigma, offsets):
    epochs = images.shape[0]
    tile = images.shape[-1]
    sky = lax.axis_size("sky")
    blocks = lax.axis_size("epoch")
    block = VELS // (blocks * lax.axis_size("vel"))
    exchange = sky == GRID_X
    rows_out = -(-(tile + 2 * REACH) // 16) * 16
    slots = LANES // MARGIN
    smem = pl.BlockSpec(memory_space=pltpu.SMEM)
    vmem = pl.BlockSpec(memory_space=pltpu.VMEM)
    dma = pltpu.SemaphoreType.DMA
    half = blocks * block
    far = max(1, (blocks - 1) * block)
    scratch = [
        pltpu.VMEM((2 * epochs, rows_out, LANES), jnp.float32),
        pltpu.VMEM((2 * epochs, rows_out, LANES), jnp.float32),
        pltpu.VMEM((rows_out, tile if exchange else tile + LANES), jnp.float32),
        pltpu.VMEM((LANES, 2 * LANES), jnp.float32),
        pltpu.VMEM((slots if exchange else 1, LANES, 2 * LANES), jnp.float32),
        pltpu.VMEM((2, 2 * LANES, 2 * LANES), jnp.bfloat16),
        pltpu.VMEM((half, 2, tile, tile), jnp.bfloat16),
        pltpu.VMEM((half, 2, tile, tile), jnp.bfloat16),
        pltpu.VMEM((far, 2, tile, tile), jnp.bfloat16),
        pltpu.VMEM((far, 2, tile, tile), jnp.bfloat16),
        pltpu.VMEM((block, 2, tile, tile), jnp.float32),
        dma((half,)), dma((half,)), dma((far,)), dma((far,)),
    ]
    if exchange:
        groups = -(-epochs // slots)
        scratch += [
            pltpu.VMEM((epochs, 2, tile, tile), jnp.bfloat16),
            pltpu.VMEM((2, 2, tile, LANES), jnp.float32),
            pltpu.VMEM((2, groups, 2, tile, LANES), jnp.bfloat16),
            pltpu.VMEM((2, groups, 2, tile, LANES), jnp.bfloat16),
            dma((2, groups)), dma((2, groups)),
        ]
        operands = (offsets, psf_sigma, valid, images, variances)
        in_specs = [smem, smem, smem, vmem, vmem]
    else:
        usable = valid[:, 0].astype(jnp.float32)[:, None, None]
        inverse = usable / variances[:, 0].astype(jnp.float32)
        scaled = images[:, 0].astype(jnp.float32) * inverse
        own = jnp.stack([scaled.astype(jnp.bfloat16), inverse.astype(jnp.bfloat16)], axis=1)
        operands = (offsets, psf_sigma) + strips(own, sky, tile)
        in_specs = [smem, smem, vmem, vmem]
    out = jax.ShapeDtypeStruct((block, 1, tile, tile), jnp.float32)
    return pl.pallas_call(
        functools.partial(fused_kernel, (tile, sky, blocks, block, epochs, exchange)),
        out_shape=(out, out),
        in_specs=in_specs,
        out_specs=(vmem, vmem),
        scratch_shapes=scratch,
        compiler_params=pltpu.CompilerParams(
            collective_id=0, has_side_effects=True, vmem_limit_bytes=56 * 2**20
        ),
    )(*operands)


def solution(mesh):
    placed = (
        P(("epoch", "vel"), ("field", "sky"), None, None),
        P(("epoch", "vel"), ("field", "sky"), None, None),
        P(("epoch", "vel"), ("field", "sky")),
        P(("field", "epoch", "vel")),
        P(None, None, "epoch"),
    )
    return jax.shard_map(
        on_device,
        mesh=mesh,
        in_specs=placed,
        out_specs=(
            P(("epoch", "vel"), ("field", "sky"), None, None),
            P(("epoch", "vel"), ("field", "sky"), None, None),
        ),
        check_vma=False,
    )
```

```python
import functools

import jax
import jax.numpy as jnp
from jax import lax
from jax.experimental import pallas as pl
from jax.experimental.pallas import tpu as pltpu
from jax.sharding import PartitionSpec as P

VELS = 16
REACH = 12
PSFR = 7
GRID_X = 4
MARGIN = REACH + PSFR
LANES = 128

phi_floor = 0.25


def shifted(block, axis, distance):
    devices = range(lax.axis_size(axis))
    route = [((i - distance) % len(devices), i) for i in devices]
    return lax.ppermute(block, axis, route)


def positions(index, tile):
    return jnp.where(
        index < tile,
        index,
        jnp.where(
            index < tile + MARGIN,
            index - tile - MARGIN,
            jnp.where(index < tile + 2 * MARGIN, index - MARGIN, 4 * tile),
        ),
    )


FAR = -1.0e9


def exponents(distance):
    away = distance.astype(jnp.float32)
    return jnp.where(jnp.abs(distance) <= PSFR, -0.5 * away * away, FAR)


def fused_kernel(plan, *refs):
    tile, sky, blocks, block, epochs, runs, exchange = plan
    if exchange:
        (offsets, sigmas, valid, images, variances, out, plane_a, plane_b, ends, row_q,
         own_q, side_q, bands, send_v, recv_v, send_x, recv_x, keep, sv, rv, sx, rx,
         own, building, sent_sides, came_sides, sz, rz) = refs
    else:
        (offsets, sigmas, own, halo, out, plane_a, plane_b, ends, row_q,
         own_q, side_q, bands, send_v, recv_v, send_x, recv_x, keep, sv, rv, sx, rx) = refs
    maps = 2
    slots = LANES // MARGIN
    rows_in = row_q.shape[1]
    rows_out = plane_a.shape[1]
    width = 2 * LANES
    mesh_id = pl.DeviceIdType.MESH
    me = lax.axis_index("sky")
    group = lax.axis_index("epoch")
    member = lax.axis_index("vel")
    column = lax.rem(lax.rem(me + GRID_X // 2, sky), GRID_X)
    before = lax.rem(me + sky - 1, sky)
    after = lax.rem(me + 1, sky)
    partner = 1 - member

    barrier = pltpu.get_barrier_semaphore()
    greeted = 1
    pl.semaphore_signal(barrier, inc=1, device_id={"vel": partner}, device_id_type=mesh_id)
    for a in range(1, blocks):
        peer = lax.rem(group + a, blocks)
        pl.semaphore_signal(barrier, inc=1, device_id={"epoch": peer}, device_id_type=mesh_id)
        greeted += 1
    if exchange:
        for other in (before, after):
            pl.semaphore_signal(barrier, inc=1, device_id={"sky": other}, device_id_type=mesh_id)
            greeted += 1

    if exchange:
        groups = sent_sides.shape[1]
        lane = lax.broadcasted_iota(jnp.int32, (tile, LANES), 1)

        def side_copy(to_after, g):
            return pltpu.make_async_remote_copy(
                src_ref=sent_sides.at[to_after, g],
                dst_ref=came_sides.at[to_after, g],
                send_sem=sz.at[to_after, g],
                recv_sem=rz.at[to_after, g],
                device_id={"sky": after if to_after else before},
                device_id_type=mesh_id,
            )

        building[...] = jnp.zeros_like(building)

        @pl.when(column == 0)
        def _():
            came_sides[1] = jnp.zeros_like(came_sides[1])

        @pl.when(column == GRID_X - 1)
        def _():
            came_sides[0] = jnp.zeros_like(came_sides[0])

        pl.semaphore_wait(barrier, greeted)

        def weigh(e, carry):
            s = lax.rem(e, slots)
            g = e // slots
            usable = valid[pl.ds(e, 1), :].astype(jnp.float32)
            inverse = usable / variances[e, 0].astype(jnp.float32)
            scaled = images[e, 0].astype(jnp.float32) * inverse
            to_slot = MARGIN * s
            to_mirror = MARGIN * (slots - 1 - s)
            for m, field in enumerate((scaled, inverse)):
                own[e, m] = field.astype(jnp.bfloat16)
                low = pltpu.roll(field, to_mirror, axis=1)
                high = pltpu.roll(field, to_slot + MARGIN, axis=1)
                at_low = (lane >= to_mirror) & (lane < to_mirror + MARGIN)
                at_high = (lane >= to_slot) & (lane < to_slot + MARGIN)
                building[0, m] = jnp.where(at_low, low, building[0, m])
                building[1, m] = jnp.where(at_high, high, building[1, m])

            @pl.when((s == slots - 1) | (e == epochs - 1))
            def _():
                sent_sides[0, g] = building[0].astype(jnp.bfloat16)
                sent_sides[1, g] = building[1].astype(jnp.bfloat16)

                @pl.when(column > 0)
                def _():
                    side_copy(0, g).start()

                @pl.when(column < GRID_X - 1)
                def _():
                    side_copy(1, g).start()

            return carry

        lax.fori_loop(0, epochs, weigh, 0)
    else:
        pl.semaphore_wait(barrier, greeted)

    shape = (rows_out, rows_in)
    row_q[...] = exponents(
        positions(lax.broadcasted_iota(jnp.int32, shape, 1), tile)
        - lax.broadcasted_iota(jnp.int32, shape, 0) + REACH
    )
    shape = (LANES, width)
    held = lax.broadcasted_iota(jnp.int32, shape, 0)
    shifted_out = lax.broadcasted_iota(jnp.int32, shape, 1) - REACH
    own_q[...] = exponents(held - shifted_out)
    if exchange:
        for s in range(slots):
            low, high = MARGIN * s, MARGIN * (slots - 1 - s)
            pixel = jnp.where(
                (held >= low) & (held < low + MARGIN),
                held - low - MARGIN,
                jnp.where((held >= high) & (held < high + MARGIN), held - high + tile, 4 * tile),
            )
            side_q[s] = exponents(pixel - shifted_out)
    else:
        side_q[0] = exponents(positions(held + tile, tile) - shifted_out)

    first = member * epochs

    def count_runs(k, carry):
        moved = []
        for e in range(epochs):
            down = jnp.abs(offsets[0, k, first + e] - offsets[0, k, first])
            moved.append(down + jnp.abs(offsets[1, k, first + e] - offsets[1, k, first]))
        for run in range(runs - 1):
            ends[k, run] = sum((at <= run).astype(jnp.int32) for at in moved)
        return carry

    lax.fori_loop(0, VELS, count_runs, 0)
    plane_a[:maps] = jnp.zeros_like(plane_a[:maps])
    plane_b[:maps] = jnp.zeros_like(plane_b[:maps])

    def correlate(e, turn):
        sigma = jnp.full((8, LANES), sigmas[e], jnp.float32)
        power = 1.0 / (sigma * sigma)
        tap = lax.broadcasted_iota(jnp.int32, (8, LANES), 1) - PSFR
        norm = jnp.sum(jnp.exp(exponents(tap) * power), axis=1, keepdims=True)
        scale = (1.0 / norm)[:1]
        power = power[:1, :1]

        def both(q):
            profile = jnp.exp(q * power) * scale
            return profile.astype(jnp.bfloat16), (profile * profile).astype(jnp.bfloat16)

        row_bands = both(row_q[...])
        s = lax.rem(e, slots) if exchange else 0
        for part, q in enumerate((own_q[...], side_q[s])):
            for m, made in enumerate(both(q)):
                bands[turn, m, part * LANES : (part + 1) * LANES] = made
        if exchange:
            g = e // slots
            lane = lax.broadcasted_iota(jnp.int32, (tile, LANES), 1)
            in_slot = (lane >= MARGIN * s) & (lane < MARGIN * s + MARGIN)
        for m in range(maps):
            if exchange:
                side = jnp.where(
                    in_slot,
                    came_sides[1, g, m].astype(jnp.float32),
                    came_sides[0, g, m].astype(jnp.float32),
                ).astype(jnp.bfloat16)
            else:
                side = halo[e, m]
            held = jnp.concatenate([own[e, m], side], axis=1)
            rows = jnp.dot(row_bands[m], held, preferred_element_type=jnp.float32)
            done = jnp.dot(
                rows.astype(jnp.bfloat16), bands[turn, m], preferred_element_type=jnp.float32
            )
            at = maps * e + m
            plane_a[at + maps] = plane_a[at] + done[:, :LANES]
            plane_b[at + maps] = plane_b[at] + done[:, LANES:]

    step = 2 if epochs % 2 == 0 and slots % 2 == 0 else 1

    def several(i, carry):
        for turn in range(step):
            correlate(step * i + turn, turn)
        return carry

    if exchange:
        for g in range(groups):

            @pl.when(column < GRID_X - 1)
            def _():
                side_copy(0, g).wait_recv()

            @pl.when(column > 0)
            def _():
                side_copy(1, g).wait_recv()

            lax.fori_loop(g * slots // step, min((g + 1) * slots, epochs) // step, several, 0)
    else:
        lax.fori_loop(0, epochs // step, several, 0)

    def vel_copy(at):
        return pltpu.make_async_remote_copy(
            src_ref=send_v.at[at], dst_ref=recv_v.at[at], send_sem=sv.at[at], recv_sem=rv.at[at],
            device_id={"vel": partner}, device_id_type=mesh_id,
        )

    def epoch_copy(at):
        peer = lax.rem(group + 1 + at // block, blocks)
        return pltpu.make_async_remote_copy(
            src_ref=send_x.at[at], dst_ref=recv_x.at[at], send_sem=sx.at[at], recv_sem=rx.at[at],
            device_id={"epoch": peer}, device_id_type=mesh_id,
        )

    def stack(slot, carry):
        a = blocks - 1 - slot // (2 * block)
        b = 1 - lax.rem(slot // block, 2)
        j = lax.rem(slot, block)
        place = a * block + j
        k = (lax.rem(group + a, blocks) * 2 + lax.rem(member + b, 2)) * block + j
        lane = lax.broadcasted_iota(jnp.int32, (tile, LANES), 1)
        summed = [jnp.zeros((tile, LANES), jnp.float32) for _ in range(maps)]
        low = jnp.zeros((), jnp.int32)
        for run in range(runs):
            high = ends[k, run] if run < runs - 1 else epochs
            at = first + jnp.minimum(low, epochs - 1)
            down = offsets[0, k, at] + REACH
            right = offsets[1, k, at] + REACH
            rows = pl.ds(down, tile)
            for m in range(maps):
                left_part = plane_a[maps * high + m, rows, :] - plane_a[maps * low + m, rows, :]
                right_part = plane_b[maps * high + m, rows, :] - plane_b[maps * low + m, rows, :]
                merged = jnp.where(lane >= right, left_part, right_part)
                summed[m] += pltpu.roll(merged, LANES - right, axis=1)
            low = high
        for m in range(maps):
            keep[j, m] = summed[m]

        @pl.when(b == 1)
        def _():
            send_v[place] = keep[j].astype(jnp.bfloat16)
            vel_copy(place).start()

        @pl.when(b == 0)
        def _():
            vel_copy(place).wait_recv()
            keep[j] = keep[j] + recv_v[place].astype(jnp.float32)

            @pl.when(a > 0)
            def _():
                send_x[place - block] = keep[j].astype(jnp.bfloat16)
                epoch_copy(place - block).start()

        return carry

    lax.fori_loop(0, 2 * blocks * block, stack, 0)

    def finish(j, carry):
        total = keep[j]
        for a in range(1, blocks):
            at = (a - 1) * block + j
            epoch_copy(at).wait_recv()
            total = total + recv_x[at].astype(jnp.float32)
        out[j] = total
        return carry

    lax.fori_loop(0, block, finish, 0)

    def drain_v(at, carry):
        vel_copy(at).wait_send()
        return carry

    lax.fori_loop(0, blocks * block, drain_v, 0)

    def drain_x(at, carry):
        epoch_copy(at).wait_send()
        return carry

    lax.fori_loop(0, (blocks - 1) * block, drain_x, 0)
    if exchange:

        def drain_z(g, carry):
            @pl.when(column > 0)
            def _():
                side_copy(0, g).wait_send()

            @pl.when(column < GRID_X - 1)
            def _():
                side_copy(1, g).wait_send()

            return carry

        lax.fori_loop(0, groups, drain_z, 0)


def strips(own, tile_count, tile):
    position = (lax.axis_index("sky") + GRID_X // 2) % tile_count
    column = position % GRID_X
    left = shifted(own[..., tile - MARGIN :], "sky", 1)
    right = shifted(own[..., :MARGIN], "sky", -1)
    left = jnp.where(column > 0, left, jnp.zeros_like(left))
    right = jnp.where(column < GRID_X - 1, right, jnp.zeros_like(right))
    blank = jnp.zeros(own.shape[:3] + (LANES - 2 * MARGIN,), jnp.bfloat16)
    both = jnp.concatenate([own, left, right, blank], axis=3)
    upper = shifted(both[:, :, tile - MARGIN :], "sky", GRID_X)
    lower = shifted(both[:, :, :MARGIN], "sky", -GRID_X)
    upper = jnp.where(position >= GRID_X, upper, jnp.zeros_like(upper))
    lower = jnp.where(position < tile_count - GRID_X, lower, jnp.zeros_like(lower))
    blank = jnp.zeros(both.shape[:2] + (LANES - 2 * MARGIN, both.shape[3]), jnp.bfloat16)
    both = jnp.concatenate([both, upper, lower, blank], axis=2)
    return both[..., :tile], both[..., tile:]


def on_device(images, variances, valid, psf_sigma, offsets):
    epochs = images.shape[0]
    tile = images.shape[-1]
    sky = lax.axis_size("sky")
    blocks = lax.axis_size("epoch")
    block = VELS // (blocks * lax.axis_size("vel"))
    exchange = sky == GRID_X
    last_epoch = epochs * blocks * lax.axis_size("vel") - 1
    runs = 1 + 2 * -(-REACH * (epochs - 1) // last_epoch)
    rows_out = -(-(tile + 2 * REACH) // 16) * 16
    slots = LANES // MARGIN
    smem = pl.BlockSpec(memory_space=pltpu.SMEM)
    vmem = pl.BlockSpec(memory_space=pltpu.VMEM)
    dma = pltpu.SemaphoreType.DMA
    half = blocks * block
    far = max(1, (blocks - 1) * block)
    scratch = [
        pltpu.VMEM((2 * (epochs + 1), rows_out, LANES), jnp.float32),
        pltpu.VMEM((2 * (epochs + 1), rows_out, LANES), jnp.float32),
        pltpu.SMEM((VELS, runs), jnp.int32),
        pltpu.VMEM((rows_out, tile if exchange else tile + LANES), jnp.float32),
        pltpu.VMEM((LANES, 2 * LANES), jnp.float32),
        pltpu.VMEM((slots if exchange else 1, LANES, 2 * LANES), jnp.float32),
        pltpu.VMEM((2, 2, 2 * LANES, 2 * LANES), jnp.bfloat16),
        pltpu.VMEM((half, 2, tile, tile), jnp.bfloat16),
        pltpu.VMEM((half, 2, tile, tile), jnp.bfloat16),
        pltpu.VMEM((far, 2, tile, tile), jnp.bfloat16),
        pltpu.VMEM((far, 2, tile, tile), jnp.bfloat16),
        pltpu.VMEM((block, 2, tile, tile), jnp.float32),
        dma((half,)), dma((half,)), dma((far,)), dma((far,)),
    ]
    if exchange:
        groups = -(-epochs // slots)
        scratch += [
            pltpu.VMEM((epochs, 2, tile, tile), jnp.bfloat16),
            pltpu.VMEM((2, 2, tile, LANES), jnp.float32),
            pltpu.VMEM((2, groups, 2, tile, LANES), jnp.bfloat16),
            pltpu.VMEM((2, groups, 2, tile, LANES), jnp.bfloat16),
            dma((2, groups)), dma((2, groups)),
        ]
        operands = (offsets, psf_sigma, valid, images, variances)
        in_specs = [smem, smem, vmem, vmem, vmem]
    else:
        usable = valid[:, 0].astype(jnp.float32)[:, None, None]
        inverse = usable / variances[:, 0].astype(jnp.float32)
        scaled = images[:, 0].astype(jnp.float32) * inverse
        own = jnp.stack([scaled.astype(jnp.bfloat16), inverse.astype(jnp.bfloat16)], axis=1)
        operands = (offsets, psf_sigma) + strips(own, sky, tile)
        in_specs = [smem, smem, vmem, vmem]
    sums = pl.pallas_call(
        functools.partial(fused_kernel, (tile, sky, blocks, block, epochs, runs, exchange)),
        out_shape=jax.ShapeDtypeStruct((block, 2, tile, tile), jnp.float32),
        in_specs=in_specs,
        out_specs=vmem,
        scratch_shapes=scratch,
        compiler_params=pltpu.CompilerParams(
            collective_id=0, has_side_effects=True, vmem_limit_bytes=56 * 2**20
        ),
    )(*operands)
    psi_sum = sums[:, 0]
    phi_sum = jnp.maximum(sums[:, 1], phi_floor)
    likelihood = psi_sum / jnp.sqrt(phi_sum)
    flux = psi_sum / phi_sum
    return (likelihood[:, None], flux[:, None])


def solution(mesh):
    placed = (
        P(("epoch", "vel"), ("field", "sky"), None, None),
        P(("epoch", "vel"), ("field", "sky"), None, None),
        P(("epoch", "vel"), ("field", "sky")),
        P(("field", "epoch", "vel")),
        P(None, None, "epoch"),
    )
    return jax.shard_map(
        on_device,
        mesh=mesh,
        in_specs=placed,
        out_specs=(
            P(("epoch", "vel"), ("field", "sky"), None, None),
            P(("epoch", "vel"), ("field", "sky"), None, None),
        ),
        check_vma=False,
    )
```

```python
import functools

import jax
import jax.numpy as jnp
from jax import lax
from jax.experimental import pallas as pl
from jax.experimental.pallas import tpu as pltpu
from jax.sharding import PartitionSpec as P

VELS = 16
REACH = 12
PSFR = 7
GRID_X = 4
MARGIN = REACH + PSFR
LANES = 128

phi_floor = 0.25


def shifted(block, axis, distance):
    devices = range(lax.axis_size(axis))
    route = [((i - distance) % len(devices), i) for i in devices]
    return lax.ppermute(block, axis, route)


def positions(index, tile):
    return jnp.where(
        index < tile,
        index,
        jnp.where(
            index < tile + MARGIN,
            index - tile - MARGIN,
            jnp.where(index < tile + 2 * MARGIN, index - MARGIN, 4 * tile),
        ),
    )


FAR = -1.0e9


def exponents(distance):
    away = distance.astype(jnp.float32)
    return jnp.where(jnp.abs(distance) <= PSFR, -0.5 * away * away, FAR)


def fused_kernel(plan, *refs):
    tile, sky, blocks, block, epochs, runs, exchange = plan
    if exchange:
        (offsets, motion, sigmas, valid, images, variances, psi_out, phi_out, plane_a, plane_b, ends, ends_made, ends_sem, row_q,
         own_q, side_q, bands, send_v, recv_v, send_x, recv_x, keep, sv, rv, sx, rx,
         own, building, sent_sides, came_sides, sz, rz) = refs
    else:
        (offsets, motion, sigmas, own, halo, psi_out, phi_out, plane_a, plane_b, ends, ends_made, ends_sem, row_q,
         own_q, side_q, bands, send_v, recv_v, send_x, recv_x, keep, sv, rv, sx, rx) = refs
    maps = 2
    slots = LANES // MARGIN
    rows_in = row_q.shape[1]
    rows_out = plane_a.shape[1]
    width = 2 * LANES
    mesh_id = pl.DeviceIdType.MESH
    me = lax.axis_index("sky")
    group = lax.axis_index("epoch")
    member = lax.axis_index("vel")
    column = lax.rem(lax.rem(me + GRID_X // 2, sky), GRID_X)
    before = lax.rem(me + sky - 1, sky)
    after = lax.rem(me + 1, sky)
    partner = 1 - member

    barrier = pltpu.get_barrier_semaphore()
    greeted = 1
    pl.semaphore_signal(barrier, inc=1, device_id={"vel": partner}, device_id_type=mesh_id)
    for a in range(1, blocks):
        peer = lax.rem(group + a, blocks)
        pl.semaphore_signal(barrier, inc=1, device_id={"epoch": peer}, device_id_type=mesh_id)
        greeted += 1
    if exchange:
        for other in (before, after):
            pl.semaphore_signal(barrier, inc=1, device_id={"sky": other}, device_id_type=mesh_id)
            greeted += 1

    if exchange:
        groups = sent_sides.shape[1]
        lane = lax.broadcasted_iota(jnp.int32, (tile, LANES), 1)

        def side_copy(to_after, g):
            return pltpu.make_async_remote_copy(
                src_ref=sent_sides.at[to_after, g],
                dst_ref=came_sides.at[to_after, g],
                send_sem=sz.at[to_after, g],
                recv_sem=rz.at[to_after, g],
                device_id={"sky": after if to_after else before},
                device_id_type=mesh_id,
            )

        building[...] = jnp.zeros_like(building)

        @pl.when(column == 0)
        def _():
            came_sides[1] = jnp.zeros_like(came_sides[1])

        @pl.when(column == GRID_X - 1)
        def _():
            came_sides[0] = jnp.zeros_like(came_sides[0])

        pl.semaphore_wait(barrier, greeted)

        def weigh(e, carry):
            s = lax.rem(e, slots)
            g = e // slots
            usable = valid[e].astype(jnp.float32)
            inverse = usable / variances[e, 0].astype(jnp.float32)
            scaled = images[e, 0].astype(jnp.float32) * inverse
            to_slot = MARGIN * s
            to_mirror = MARGIN * (slots - 1 - s)
            for m, field in enumerate((scaled, inverse)):
                own[e, m] = field.astype(jnp.bfloat16)
                low = pltpu.roll(field, to_mirror, axis=1)
                high = pltpu.roll(field, to_slot + MARGIN, axis=1)
                at_low = (lane >= to_mirror) & (lane < to_mirror + MARGIN)
                at_high = (lane >= to_slot) & (lane < to_slot + MARGIN)
                building[0, m] = jnp.where(at_low, low, building[0, m])
                building[1, m] = jnp.where(at_high, high, building[1, m])

            @pl.when((s == slots - 1) | (e == epochs - 1))
            def _():
                sent_sides[0, g] = building[0].astype(jnp.bfloat16)
                sent_sides[1, g] = building[1].astype(jnp.bfloat16)

                @pl.when(column > 0)
                def _():
                    side_copy(0, g).start()

                @pl.when(column < GRID_X - 1)
                def _():
                    side_copy(1, g).start()

            return carry

        lax.fori_loop(0, epochs, weigh, 0)
    else:
        pl.semaphore_wait(barrier, greeted)

    shape = (rows_out, rows_in)
    row_q[...] = exponents(
        positions(lax.broadcasted_iota(jnp.int32, shape, 1), tile)
        - lax.broadcasted_iota(jnp.int32, shape, 0) + REACH
    )
    shape = (LANES, width)
    held = lax.broadcasted_iota(jnp.int32, shape, 0)
    shifted_out = lax.broadcasted_iota(jnp.int32, shape, 1) - REACH
    own_q[...] = exponents(held - shifted_out)
    if exchange:
        for s in range(slots):
            low, high = MARGIN * s, MARGIN * (slots - 1 - s)
            pixel = jnp.where(
                (held >= low) & (held < low + MARGIN),
                held - low - MARGIN,
                jnp.where((held >= high) & (held < high + MARGIN), held - high + tile, 4 * tile),
            )
            side_q[s] = exponents(pixel - shifted_out)
    else:
        side_q[0] = exponents(positions(held + tile, tile) - shifted_out)

    first = member * epochs

    at_epoch = lax.broadcasted_iota(jnp.int32, motion.shape[1:], 1)
    moved = jnp.zeros(motion.shape[1:], jnp.int32)
    for way in range(2):
        start = jnp.where(at_epoch == first, motion[way], 0)
        moved += jnp.abs(motion[way] - jnp.sum(start, axis=1, keepdims=True))
    held_here = (at_epoch >= first) & (at_epoch < first + epochs)
    counted = jnp.zeros(ends_made.shape, jnp.int32)
    at_run = lax.broadcasted_iota(jnp.int32, ends_made.shape, 1)
    for run in range(runs - 1):
        count = jnp.sum((held_here & (moved <= run)).astype(jnp.int32), axis=1, keepdims=True)
        counted = jnp.where(at_run == run, count, counted)
    ends_made[...] = counted
    ends_copy = pltpu.make_async_copy(ends_made, ends, ends_sem)
    ends_copy.start()
    plane_a[:maps] = jnp.zeros_like(plane_a[:maps])
    plane_b[:maps] = jnp.zeros_like(plane_b[:maps])

    def correlate(e, turn):
        sigma = jnp.full((8, LANES), sigmas[e], jnp.float32)
        power = 1.0 / (sigma * sigma)
        tap = lax.broadcasted_iota(jnp.int32, (8, LANES), 1) - PSFR
        norm = jnp.sum(jnp.exp(exponents(tap) * power), axis=1, keepdims=True)
        scale = (1.0 / norm)[:1]
        power = power[:1, :1]

        def both(q):
            profile = jnp.exp(q * power) * scale
            return profile.astype(jnp.bfloat16), (profile * profile).astype(jnp.bfloat16)

        row_bands = both(row_q[...])
        s = lax.rem(e, slots) if exchange else 0
        for part, q in enumerate((own_q[...], side_q[s])):
            for m, made in enumerate(both(q)):
                bands[turn, m, part * LANES : (part + 1) * LANES] = made
        if exchange:
            g = e // slots
            lane = lax.broadcasted_iota(jnp.int32, (tile, LANES), 1)
            in_slot = (lane >= MARGIN * s) & (lane < MARGIN * s + MARGIN)
        for m in range(maps):
            if exchange:
                side = jnp.where(
                    in_slot,
                    came_sides[1, g, m].astype(jnp.float32),
                    came_sides[0, g, m].astype(jnp.float32),
                ).astype(jnp.bfloat16)
            else:
                side = halo[e, m]
            held = jnp.concatenate([own[e, m], side], axis=1)
            rows = jnp.dot(row_bands[m], held, preferred_element_type=jnp.float32)
            done = jnp.dot(
                rows.astype(jnp.bfloat16), bands[turn, m], preferred_element_type=jnp.float32
            )
            at = maps * e + m
            plane_a[at + maps] = plane_a[at] + done[:, :LANES]
            plane_b[at + maps] = plane_b[at] + done[:, LANES:]

    step = 2 if epochs % 2 == 0 and slots % 2 == 0 else 1

    def several(i, carry):
        for turn in range(step):
            correlate(step * i + turn, turn)
        return carry

    if exchange:
        for g in range(groups):

            @pl.when(column < GRID_X - 1)
            def _():
                side_copy(0, g).wait_recv()

            @pl.when(column > 0)
            def _():
                side_copy(1, g).wait_recv()

            lax.fori_loop(g * slots // step, min((g + 1) * slots, epochs) // step, several, 0)
    else:
        lax.fori_loop(0, epochs // step, several, 0)

    def vel_copy(at):
        return pltpu.make_async_remote_copy(
            src_ref=send_v.at[at], dst_ref=recv_v.at[at], send_sem=sv.at[at], recv_sem=rv.at[at],
            device_id={"vel": partner}, device_id_type=mesh_id,
        )

    def epoch_copy(at):
        peer = lax.rem(group + 1 + at // block, blocks)
        return pltpu.make_async_remote_copy(
            src_ref=send_x.at[at], dst_ref=recv_x.at[at], send_sem=sx.at[at], recv_sem=rx.at[at],
            device_id={"epoch": peer}, device_id_type=mesh_id,
        )

    def stack(slot, carry):
        a = blocks - 1 - slot // (2 * block)
        turn = lax.rem(slot, 2 * block)
        mine = ((turn > 0) & (lax.rem(turn, 2) == 0)) | (turn == 2 * block - 1)
        b = jnp.where(mine, 0, 1)
        j = jnp.where(turn == 2 * block - 1, block - 1, jnp.where(mine, turn // 2 - 1, (turn + 1) // 2))
        place = a * block + j
        k = (lax.rem(group + a, blocks) * 2 + lax.rem(member + b, 2)) * block + j
        lane = lax.broadcasted_iota(jnp.int32, (tile, LANES), 1)
        summed = [jnp.zeros((tile, LANES), jnp.float32) for _ in range(maps)]
        low = jnp.zeros((), jnp.int32)
        for run in range(runs):
            high = ends[k, run] if run < runs - 1 else epochs
            at = first + jnp.minimum(low, epochs - 1)
            down = offsets[0, k, at] + REACH
            right = offsets[1, k, at] + REACH
            rows = pl.ds(down, tile)
            for m in range(maps):
                left_part = plane_a[maps * high + m, rows, :] - plane_a[maps * low + m, rows, :]
                right_part = plane_b[maps * high + m, rows, :] - plane_b[maps * low + m, rows, :]
                merged = jnp.where(lane >= right, left_part, right_part)
                summed[m] += pltpu.roll(merged, LANES - right, axis=1)
            low = high
        for m in range(maps):
            keep[b, j, m] = summed[m]

        @pl.when(b == 1)
        def _():
            send_v[place] = keep[1, j].astype(jnp.bfloat16)
            vel_copy(place).start()

        @pl.when(b == 0)
        def _():
            vel_copy(place).wait_recv()
            keep[0, j] = keep[0, j] + recv_v[place].astype(jnp.float32)

            @pl.when(a > 0)
            def _():
                send_x[place - block] = keep[0, j].astype(jnp.bfloat16)
                epoch_copy(place - block).start()

        return carry

    ends_copy.wait()
    lax.fori_loop(0, 2 * blocks * block, stack, 0)

    def finish(j, carry):
        total = keep[0, j]
        for a in range(1, blocks):
            at = (a - 1) * block + j
            epoch_copy(at).wait_recv()
            total = total + recv_x[at].astype(jnp.float32)
        psi_out[j] = total[0]
        phi_out[j] = total[1]
        return carry

    lax.fori_loop(0, block, finish, 0)

    def drain_v(at, carry):
        vel_copy(at).wait_send()
        return carry

    lax.fori_loop(0, blocks * block, drain_v, 0)

    def drain_x(at, carry):
        epoch_copy(at).wait_send()
        return carry

    lax.fori_loop(0, (blocks - 1) * block, drain_x, 0)
    if exchange:

        def drain_z(g, carry):
            @pl.when(column > 0)
            def _():
                side_copy(0, g).wait_send()

            @pl.when(column < GRID_X - 1)
            def _():
                side_copy(1, g).wait_send()

            return carry

        lax.fori_loop(0, groups, drain_z, 0)


def strips(own, tile_count, tile):
    position = (lax.axis_index("sky") + GRID_X // 2) % tile_count
    column = position % GRID_X
    left = shifted(own[..., tile - MARGIN :], "sky", 1)
    right = shifted(own[..., :MARGIN], "sky", -1)
    left = jnp.where(column > 0, left, jnp.zeros_like(left))
    right = jnp.where(column < GRID_X - 1, right, jnp.zeros_like(right))
    blank = jnp.zeros(own.shape[:3] + (LANES - 2 * MARGIN,), jnp.bfloat16)
    both = jnp.concatenate([own, left, right, blank], axis=3)
    upper = shifted(both[:, :, tile - MARGIN :], "sky", GRID_X)
    lower = shifted(both[:, :, :MARGIN], "sky", -GRID_X)
    upper = jnp.where(position >= GRID_X, upper, jnp.zeros_like(upper))
    lower = jnp.where(position < tile_count - GRID_X, lower, jnp.zeros_like(lower))
    blank = jnp.zeros(both.shape[:2] + (LANES - 2 * MARGIN, both.shape[3]), jnp.bfloat16)
    both = jnp.concatenate([both, upper, lower, blank], axis=2)
    return both[..., :tile], both[..., tile:]


def on_device(images, variances, valid, psf_sigma, offsets):
    epochs = images.shape[0]
    tile = images.shape[-1]
    sky = lax.axis_size("sky")
    blocks = lax.axis_size("epoch")
    block = VELS // (blocks * lax.axis_size("vel"))
    exchange = sky == GRID_X
    last_epoch = epochs * blocks * lax.axis_size("vel") - 1
    runs = 1 + 2 * -(-REACH * (epochs - 1) // last_epoch)
    rows_out = -(-(tile + 2 * REACH) // 16) * 16
    slots = LANES // MARGIN
    smem = pl.BlockSpec(memory_space=pltpu.SMEM)
    vmem = pl.BlockSpec(memory_space=pltpu.VMEM)
    dma = pltpu.SemaphoreType.DMA
    half = blocks * block
    far = max(1, (blocks - 1) * block)
    scratch = [
        pltpu.VMEM((2 * (epochs + 1), rows_out, LANES), jnp.float32),
        pltpu.VMEM((2 * (epochs + 1), rows_out, LANES), jnp.float32),
        pltpu.SMEM((VELS, LANES), jnp.int32),
        pltpu.VMEM((VELS, LANES), jnp.int32),
        dma(()),
        pltpu.VMEM((rows_out, tile if exchange else tile + LANES), jnp.float32),
        pltpu.VMEM((LANES, 2 * LANES), jnp.float32),
        pltpu.VMEM((slots if exchange else 1, LANES, 2 * LANES), jnp.float32),
        pltpu.VMEM((2, 2, 2 * LANES, 2 * LANES), jnp.bfloat16),
        pltpu.VMEM((half, 2, tile, tile), jnp.bfloat16),
        pltpu.VMEM((half, 2, tile, tile), jnp.bfloat16),
        pltpu.VMEM((far, 2, tile, tile), jnp.bfloat16),
        pltpu.VMEM((far, 2, tile, tile), jnp.bfloat16),
        pltpu.VMEM((2, block, 2, tile, tile), jnp.float32),
        dma((half,)), dma((half,)), dma((far,)), dma((far,)),
    ]
    if exchange:
        groups = -(-epochs // slots)
        scratch += [
            pltpu.VMEM((epochs, 2, tile, tile), jnp.bfloat16),
            pltpu.VMEM((2, 2, tile, LANES), jnp.float32),
            pltpu.VMEM((2, groups, 2, tile, LANES), jnp.bfloat16),
            pltpu.VMEM((2, groups, 2, tile, LANES), jnp.bfloat16),
            dma((2, groups)), dma((2, groups)),
        ]
        operands = (offsets, offsets, psf_sigma, valid.reshape(epochs), images, variances)
        in_specs = [smem, vmem, smem, smem, vmem, vmem]
    else:
        usable = valid[:, 0].astype(jnp.float32)[:, None, None]
        inverse = usable / variances[:, 0].astype(jnp.float32)
        scaled = images[:, 0].astype(jnp.float32) * inverse
        own = jnp.stack([scaled.astype(jnp.bfloat16), inverse.astype(jnp.bfloat16)], axis=1)
        operands = (offsets, offsets, psf_sigma) + strips(own, sky, tile)
        in_specs = [smem, vmem, smem, vmem, vmem]
    out = jax.ShapeDtypeStruct((block, tile, tile), jnp.float32)
    psi_sum, phi_sum = pl.pallas_call(
        functools.partial(fused_kernel, (tile, sky, blocks, block, epochs, runs, exchange)),
        out_shape=(out, out),
        in_specs=in_specs,
        out_specs=(vmem, vmem),
        scratch_shapes=scratch,
        compiler_params=pltpu.CompilerParams(
            collective_id=0, has_side_effects=True, vmem_limit_bytes=56 * 2**20
        ),
    )(*operands)
    phi_sum = jnp.maximum(phi_sum, phi_floor)
    likelihood = psi_sum / jnp.sqrt(phi_sum)
    flux = psi_sum / phi_sum
    return (likelihood[:, None], flux[:, None])


def solution(mesh):
    placed = (
        P(("epoch", "vel"), ("field", "sky"), None, None),
        P(("epoch", "vel"), ("field", "sky"), None, None),
        P(("epoch", "vel"), ("field", "sky")),
        P(("field", "epoch", "vel")),
        P(None, None, "epoch"),
    )
    return jax.shard_map(
        on_device,
        mesh=mesh,
        in_specs=placed,
        out_specs=(
            P(("epoch", "vel"), ("field", "sky"), None, None),
            P(("epoch", "vel"), ("field", "sky"), None, None),
        ),
        check_vma=False,
    )
```

```python
import functools

import jax
import jax.numpy as jnp
from jax import lax
from jax.experimental import pallas as pl
from jax.experimental.pallas import tpu as pltpu
from jax.sharding import PartitionSpec as P

VELS = 16
REACH = 12
PSFR = 7
GRID_X = 4
MARGIN = REACH + PSFR
LANES = 128

phi_floor = 0.25


def shifted(block, axis, distance):
    devices = range(lax.axis_size(axis))
    route = [((i - distance) % len(devices), i) for i in devices]
    return lax.ppermute(block, axis, route)


def positions(index, tile):
    return jnp.where(
        index < tile,
        index,
        jnp.where(
            index < tile + MARGIN,
            index - tile - MARGIN,
            jnp.where(index < tile + 2 * MARGIN, index - MARGIN, 4 * tile),
        ),
    )


FAR = -1.0e9


def exponents(distance):
    away = distance.astype(jnp.float32)
    return jnp.where(jnp.abs(distance) <= PSFR, -0.5 * away * away, FAR)


def fused_kernel(plan, *refs):
    tile, sky, blocks, block, epochs, runs, widths, exchange = plan
    if exchange:
        (offsets, motion, sigmas, valid, images, variances, psi_out, phi_out, plane_a, plane_b, ends, ends_made, ends_sem, row_q,
         own_q, side_q, bands, send_v, recv_v, send_x, recv_x, keep, sv, rv, sx, rx,
         own, building, sent_sides, came_sides, sz, rz) = refs
    else:
        (offsets, motion, sigmas, own, halo, psi_out, phi_out, plane_a, plane_b, ends, ends_made, ends_sem, row_q,
         own_q, side_q, bands, send_v, recv_v, send_x, recv_x, keep, sv, rv, sx, rx) = refs
    maps = 2
    rows_in = row_q.shape[1]
    rows_out = plane_a.shape[1]
    width = 2 * LANES
    mesh_id = pl.DeviceIdType.MESH
    me = lax.axis_index("sky")
    group = lax.axis_index("epoch")
    member = lax.axis_index("vel")
    column = lax.rem(lax.rem(me + GRID_X // 2, sky), GRID_X)
    before = lax.rem(me + sky - 1, sky)
    after = lax.rem(me + 1, sky)
    partner = 1 - member

    if exchange:
        wide, slots = widths[0]
        for at, (each_wide, each_slots) in enumerate(widths):
            here = 2 * group + member == at
            wide = jnp.where(here, each_wide, wide)
            slots = jnp.where(here, each_slots, slots)

    barrier = pltpu.get_barrier_semaphore()
    greeted = 1
    pl.semaphore_signal(barrier, inc=1, device_id={"vel": partner}, device_id_type=mesh_id)
    for a in range(1, blocks):
        peer = lax.rem(group + a, blocks)
        pl.semaphore_signal(barrier, inc=1, device_id={"epoch": peer}, device_id_type=mesh_id)
        greeted += 1
    if exchange:
        for other in (before, after):
            pl.semaphore_signal(barrier, inc=1, device_id={"sky": other}, device_id_type=mesh_id)
            greeted += 1

    if exchange:
        groups = sent_sides.shape[1]
        lane = lax.broadcasted_iota(jnp.int32, (tile, LANES), 1)

        def side_copy(to_after, g):
            return pltpu.make_async_remote_copy(
                src_ref=sent_sides.at[to_after, g],
                dst_ref=came_sides.at[to_after, g],
                send_sem=sz.at[to_after, g],
                recv_sem=rz.at[to_after, g],
                device_id={"sky": after if to_after else before},
                device_id_type=mesh_id,
            )

        building[...] = jnp.zeros_like(building)

        @pl.when(column == 0)
        def _():
            came_sides[1] = jnp.zeros_like(came_sides[1])

        @pl.when(column == GRID_X - 1)
        def _():
            came_sides[0] = jnp.zeros_like(came_sides[0])

        pl.semaphore_wait(barrier, greeted)

        def weigh(e, carry):
            s = lax.rem(e, slots)
            g = e // slots
            usable = valid[e].astype(jnp.float32)
            inverse = usable / variances[e, 0].astype(jnp.float32)
            scaled = images[e, 0].astype(jnp.float32) * inverse
            to_slot = wide * s
            to_mirror = wide * (slots - 1 - s)
            for m, field in enumerate((scaled, inverse)):
                own[e, m] = field.astype(jnp.bfloat16)
                low = pltpu.roll(field, to_mirror, axis=1)
                high = pltpu.roll(field, lax.rem(to_slot + wide, LANES), axis=1)
                at_low = (lane >= to_mirror) & (lane < to_mirror + wide)
                at_high = (lane >= to_slot) & (lane < to_slot + wide)
                building[0, m] = jnp.where(at_low, low, building[0, m])
                building[1, m] = jnp.where(at_high, high, building[1, m])

            @pl.when((s == slots - 1) | (e == epochs - 1))
            def _():
                sent_sides[0, g] = building[0].astype(jnp.bfloat16)
                sent_sides[1, g] = building[1].astype(jnp.bfloat16)

                @pl.when(column > 0)
                def _():
                    side_copy(0, g).start()

                @pl.when(column < GRID_X - 1)
                def _():
                    side_copy(1, g).start()

            return carry

        lax.fori_loop(0, epochs, weigh, 0)
    else:
        pl.semaphore_wait(barrier, greeted)

    shape = (rows_out, rows_in)
    row_q[...] = exponents(
        positions(lax.broadcasted_iota(jnp.int32, shape, 1), tile)
        - lax.broadcasted_iota(jnp.int32, shape, 0) + REACH
    )
    shape = (LANES, width)
    held = lax.broadcasted_iota(jnp.int32, shape, 0)
    shifted_out = lax.broadcasted_iota(jnp.int32, shape, 1) - REACH
    own_q[...] = exponents(held - shifted_out)
    if exchange:

        def place_strips(s, carry):
            low, high = wide * s, wide * (slots - 1 - s)
            pixel = jnp.where(
                (held >= low) & (held < low + wide),
                held - low - wide,
                jnp.where((held >= high) & (held < high + wide), held - high + tile, 4 * tile),
            )
            side_q[s] = exponents(pixel - shifted_out)
            return carry

        lax.fori_loop(0, slots, place_strips, 0)
    else:
        side_q[0] = exponents(positions(held + tile, tile) - shifted_out)

    first = member * epochs

    at_epoch = lax.broadcasted_iota(jnp.int32, motion.shape[1:], 1)
    moved = jnp.zeros(motion.shape[1:], jnp.int32)
    for way in range(2):
        start = jnp.where(at_epoch == first, motion[way], 0)
        moved += jnp.abs(motion[way] - jnp.sum(start, axis=1, keepdims=True))
    held_here = (at_epoch >= first) & (at_epoch < first + epochs)
    counted = jnp.zeros(ends_made.shape, jnp.int32)
    at_run = lax.broadcasted_iota(jnp.int32, ends_made.shape, 1)
    for run in range(runs - 1):
        count = jnp.sum((held_here & (moved <= run)).astype(jnp.int32), axis=1, keepdims=True)
        counted = jnp.where(at_run == run, count, counted)
    ends_made[...] = counted
    ends_copy = pltpu.make_async_copy(ends_made, ends, ends_sem)
    ends_copy.start()
    plane_a[:maps] = jnp.zeros_like(plane_a[:maps])
    plane_b[:maps] = jnp.zeros_like(plane_b[:maps])

    def correlate(e, turn):
        sigma = jnp.full((8, LANES), sigmas[e], jnp.float32)
        power = 1.0 / (sigma * sigma)
        tap = lax.broadcasted_iota(jnp.int32, (8, LANES), 1) - PSFR
        norm = jnp.sum(jnp.exp(exponents(tap) * power), axis=1, keepdims=True)
        scale = (1.0 / norm)[:1]
        power = power[:1, :1]

        def both(q):
            profile = jnp.exp(q * power) * scale
            return profile.astype(jnp.bfloat16), (profile * profile).astype(jnp.bfloat16)

        row_bands = both(row_q[...])
        s = lax.rem(e, slots) if exchange else 0
        for part, q in enumerate((own_q[...], side_q[s])):
            for m, made in enumerate(both(q)):
                bands[turn, m, part * LANES : (part + 1) * LANES] = made
        if exchange:
            g = e // slots
            lane = lax.broadcasted_iota(jnp.int32, (tile, LANES), 1)
            in_slot = (lane >= wide * s) & (lane < wide * s + wide)
        for m in range(maps):
            if exchange:
                side = jnp.where(
                    in_slot,
                    came_sides[1, g, m].astype(jnp.float32),
                    came_sides[0, g, m].astype(jnp.float32),
                ).astype(jnp.bfloat16)
            else:
                side = halo[e, m]
            held = jnp.concatenate([own[e, m], side], axis=1)
            rows = jnp.dot(row_bands[m], held, preferred_element_type=jnp.float32)
            done = jnp.dot(
                rows.astype(jnp.bfloat16), bands[turn, m], preferred_element_type=jnp.float32
            )
            at = maps * e + m
            plane_a[at + maps] = plane_a[at] + done[:, :LANES]
            plane_b[at + maps] = plane_b[at] + done[:, LANES:]

    step = 2 if epochs % 2 == 0 else 1

    def several(i, carry):
        for turn in range(step):
            correlate(step * i + turn, turn)
        return carry

    if exchange:
        for g in range(groups):

            @pl.when((column < GRID_X - 1) & (g * slots < epochs))
            def _():
                side_copy(0, g).wait_recv()

            @pl.when((column > 0) & (g * slots < epochs))
            def _():
                side_copy(1, g).wait_recv()

            begin = jnp.minimum(g * slots, epochs) // step
            end = jnp.minimum((g + 1) * slots, epochs) // step
            lax.fori_loop(begin, end, several, 0)
    else:
        lax.fori_loop(0, epochs // step, several, 0)

    def vel_copy(at):
        return pltpu.make_async_remote_copy(
            src_ref=send_v.at[at], dst_ref=recv_v.at[at], send_sem=sv.at[at], recv_sem=rv.at[at],
            device_id={"vel": partner}, device_id_type=mesh_id,
        )

    def epoch_copy(at):
        peer = lax.rem(group + 1 + at // block, blocks)
        return pltpu.make_async_remote_copy(
            src_ref=send_x.at[at], dst_ref=recv_x.at[at], send_sem=sx.at[at], recv_sem=rx.at[at],
            device_id={"epoch": peer}, device_id_type=mesh_id,
        )

    def stack(slot, carry):
        a = blocks - 1 - slot // (2 * block)
        turn = lax.rem(slot, 2 * block)
        mine = ((turn > 0) & (lax.rem(turn, 2) == 0)) | (turn == 2 * block - 1)
        b = jnp.where(mine, 0, 1)
        j = jnp.where(turn == 2 * block - 1, block - 1, jnp.where(mine, turn // 2 - 1, (turn + 1) // 2))
        place = a * block + j
        k = (lax.rem(group + a, blocks) * 2 + lax.rem(member + b, 2)) * block + j
        lane = lax.broadcasted_iota(jnp.int32, (tile, LANES), 1)
        summed = [jnp.zeros((tile, LANES), jnp.float32) for _ in range(maps)]
        low = jnp.zeros((), jnp.int32)
        for run in range(runs):
            high = ends[k, run] if run < runs - 1 else epochs
            at = first + jnp.minimum(low, epochs - 1)
            down = offsets[0, k, at] + REACH
            right = offsets[1, k, at] + REACH
            rows = pl.ds(down, tile)
            for m in range(maps):
                left_part = plane_a[maps * high + m, rows, :] - plane_a[maps * low + m, rows, :]
                right_part = plane_b[maps * high + m, rows, :] - plane_b[maps * low + m, rows, :]
                merged = jnp.where(lane >= right, left_part, right_part)
                summed[m] += pltpu.roll(merged, LANES - right, axis=1)
            low = high
        for m in range(maps):
            keep[b, j, m] = summed[m]

        @pl.when(b == 1)
        def _():
            send_v[place] = keep[1, j].astype(jnp.bfloat16)
            vel_copy(place).start()

        @pl.when(b == 0)
        def _():
            vel_copy(place).wait_recv()
            keep[0, j] = keep[0, j] + recv_v[place].astype(jnp.float32)

            @pl.when(a > 0)
            def _():
                send_x[place - block] = keep[0, j].astype(jnp.bfloat16)
                epoch_copy(place - block).start()

        return carry

    ends_copy.wait()
    lax.fori_loop(0, 2 * blocks * block, stack, 0)

    def finish(j, carry):
        total = keep[0, j]
        for a in range(1, blocks):
            at = (a - 1) * block + j
            epoch_copy(at).wait_recv()
            total = total + recv_x[at].astype(jnp.float32)
        psi_out[j] = total[0]
        phi_out[j] = total[1]
        return carry

    lax.fori_loop(0, block, finish, 0)

    def drain_v(at, carry):
        vel_copy(at).wait_send()
        return carry

    lax.fori_loop(0, blocks * block, drain_v, 0)

    def drain_x(at, carry):
        epoch_copy(at).wait_send()
        return carry

    lax.fori_loop(0, (blocks - 1) * block, drain_x, 0)
    if exchange:

        def drain_z(g, carry):
            @pl.when((column > 0) & (g * slots < epochs))
            def _():
                side_copy(0, g).wait_send()

            @pl.when((column < GRID_X - 1) & (g * slots < epochs))
            def _():
                side_copy(1, g).wait_send()

            return carry

        lax.fori_loop(0, groups, drain_z, 0)


def strips(own, tile_count, tile):
    position = (lax.axis_index("sky") + GRID_X // 2) % tile_count
    column = position % GRID_X
    left = shifted(own[..., tile - MARGIN :], "sky", 1)
    right = shifted(own[..., :MARGIN], "sky", -1)
    left = jnp.where(column > 0, left, jnp.zeros_like(left))
    right = jnp.where(column < GRID_X - 1, right, jnp.zeros_like(right))
    blank = jnp.zeros(own.shape[:3] + (LANES - 2 * MARGIN,), jnp.bfloat16)
    both = jnp.concatenate([own, left, right, blank], axis=3)
    upper = shifted(both[:, :, tile - MARGIN :], "sky", GRID_X)
    lower = shifted(both[:, :, :MARGIN], "sky", -GRID_X)
    upper = jnp.where(position >= GRID_X, upper, jnp.zeros_like(upper))
    lower = jnp.where(position < tile_count - GRID_X, lower, jnp.zeros_like(lower))
    blank = jnp.zeros(both.shape[:2] + (LANES - 2 * MARGIN, both.shape[3]), jnp.bfloat16)
    both = jnp.concatenate([both, upper, lower, blank], axis=2)
    return both[..., :tile], both[..., tile:]


def on_device(images, variances, valid, psf_sigma, offsets):
    epochs = images.shape[0]
    tile = images.shape[-1]
    sky = lax.axis_size("sky")
    blocks = lax.axis_size("epoch")
    block = VELS // (blocks * lax.axis_size("vel"))
    exchange = sky == GRID_X
    last_epoch = epochs * blocks * lax.axis_size("vel") - 1
    runs = 1 + 2 * -(-REACH * (epochs - 1) // last_epoch)
    rows_out = -(-(tile + 2 * REACH) // 16) * 16
    devices = blocks * lax.axis_size("vel")
    reaches = [PSFR + -(-REACH * ((at + 1) * epochs - 1) // last_epoch) for at in range(devices)]
    widths = [(wide, LANES // wide // 2 * 2) for wide in reaches]
    slots = max(each for _, each in widths)
    smem = pl.BlockSpec(memory_space=pltpu.SMEM)
    vmem = pl.BlockSpec(memory_space=pltpu.VMEM)
    dma = pltpu.SemaphoreType.DMA
    half = blocks * block
    far = max(1, (blocks - 1) * block)
    scratch = [
        pltpu.VMEM((2 * (epochs + 1), rows_out, LANES), jnp.float32),
        pltpu.VMEM((2 * (epochs + 1), rows_out, LANES), jnp.float32),
        pltpu.SMEM((VELS, LANES), jnp.int32),
        pltpu.VMEM((VELS, LANES), jnp.int32),
        dma(()),
        pltpu.VMEM((rows_out, tile if exchange else tile + LANES), jnp.float32),
        pltpu.VMEM((LANES, 2 * LANES), jnp.float32),
        pltpu.VMEM((slots if exchange else 1, LANES, 2 * LANES), jnp.float32),
        pltpu.VMEM((2, 2, 2 * LANES, 2 * LANES), jnp.bfloat16),
        pltpu.VMEM((half, 2, tile, tile), jnp.bfloat16),
        pltpu.VMEM((half, 2, tile, tile), jnp.bfloat16),
        pltpu.VMEM((far, 2, tile, tile), jnp.bfloat16),
        pltpu.VMEM((far, 2, tile, tile), jnp.bfloat16),
        pltpu.VMEM((2, block, 2, tile, tile), jnp.float32),
        dma((half,)), dma((half,)), dma((far,)), dma((far,)),
    ]
    if exchange:
        groups = -(-epochs // min(each for _, each in widths))
        scratch += [
            pltpu.VMEM((epochs, 2, tile, tile), jnp.bfloat16),
            pltpu.VMEM((2, 2, tile, LANES), jnp.float32),
            pltpu.VMEM((2, groups, 2, tile, LANES), jnp.bfloat16),
            pltpu.VMEM((2, groups, 2, tile, LANES), jnp.bfloat16),
            dma((2, groups)), dma((2, groups)),
        ]
        operands = (offsets, offsets, psf_sigma, valid.reshape(epochs), images, variances)
        in_specs = [smem, vmem, smem, smem, vmem, vmem]
    else:
        usable = valid[:, 0].astype(jnp.float32)[:, None, None]
        inverse = usable / variances[:, 0].astype(jnp.float32)
        scaled = images[:, 0].astype(jnp.float32) * inverse
        own = jnp.stack([scaled.astype(jnp.bfloat16), inverse.astype(jnp.bfloat16)], axis=1)
        operands = (offsets, offsets, psf_sigma) + strips(own, sky, tile)
        in_specs = [smem, vmem, smem, vmem, vmem]
    out = jax.ShapeDtypeStruct((block, tile, tile), jnp.float32)
    psi_sum, phi_sum = pl.pallas_call(
        functools.partial(fused_kernel, (tile, sky, blocks, block, epochs, runs, widths, exchange)),
        out_shape=(out, out),
        in_specs=in_specs,
        out_specs=(vmem, vmem),
        scratch_shapes=scratch,
        compiler_params=pltpu.CompilerParams(
            collective_id=0, has_side_effects=True, vmem_limit_bytes=56 * 2**20
        ),
    )(*operands)
    phi_sum = jnp.maximum(phi_sum, phi_floor)
    likelihood = psi_sum / jnp.sqrt(phi_sum)
    flux = psi_sum / phi_sum
    return (likelihood[:, None], flux[:, None])


def solution(mesh):
    placed = (
        P(("epoch", "vel"), ("field", "sky"), None, None),
        P(("epoch", "vel"), ("field", "sky"), None, None),
        P(("epoch", "vel"), ("field", "sky")),
        P(("field", "epoch", "vel")),
        P(None, None, "epoch"),
    )
    return jax.shard_map(
        on_device,
        mesh=mesh,
        in_specs=placed,
        out_specs=(
            P(("epoch", "vel"), ("field", "sky"), None, None),
            P(("epoch", "vel"), ("field", "sky"), None, None),
        ),
        check_vma=False,
    )
```

```python
import functools

import jax
import jax.numpy as jnp
from jax import lax
from jax.experimental import pallas as pl
from jax.experimental.pallas import tpu as pltpu
from jax.sharding import PartitionSpec as P

VELS = 16
REACH = 12
PSFR = 7
GRID_X = 4
MARGIN = REACH + PSFR
LANES = 128

phi_floor = 0.25


def shifted(block, axis, distance):
    devices = range(lax.axis_size(axis))
    route = [((i - distance) % len(devices), i) for i in devices]
    return lax.ppermute(block, axis, route)


def positions(index, tile):
    return jnp.where(
        index < tile,
        index,
        jnp.where(
            index < tile + MARGIN,
            index - tile - MARGIN,
            jnp.where(index < tile + 2 * MARGIN, index - MARGIN, 4 * tile),
        ),
    )


FAR = -1.0e9


def exponents(distance):
    away = distance.astype(jnp.float32)
    return jnp.where(jnp.abs(distance) <= PSFR, -0.5 * away * away, FAR)


def fused_kernel(plan, *refs):
    tile, sky, blocks, block, epochs, runs, widths, exchange = plan
    if exchange:
        (offsets, motion, sigmas, valid, images, variances, psi_out, phi_out, plane_a, plane_b, ends, ends_made, ends_sem, row_q,
         own_q, side_q, bands, send_v, recv_v, send_x, recv_x, keep, sv, rv, sx, rx,
         own, building, sent_sides, came_sides, sz, rz) = refs
    else:
        (offsets, motion, sigmas, own, halo, psi_out, phi_out, plane_a, plane_b, ends, ends_made, ends_sem, row_q,
         own_q, side_q, bands, send_v, recv_v, send_x, recv_x, keep, sv, rv, sx, rx) = refs
    maps = 2
    rows_in = row_q.shape[1]
    rows_out = plane_a.shape[1]
    width = 2 * LANES
    mesh_id = pl.DeviceIdType.MESH
    me = lax.axis_index("sky")
    group = lax.axis_index("epoch")
    member = lax.axis_index("vel")
    column = lax.rem(lax.rem(me + GRID_X // 2, sky), GRID_X)
    before = lax.rem(me + sky - 1, sky)
    after = lax.rem(me + 1, sky)
    partner = 1 - member

    if exchange:
        wide, slots = widths[0]
        for at, (each_wide, each_slots) in enumerate(widths):
            here = 2 * group + member == at
            wide = jnp.where(here, each_wide, wide)
            slots = jnp.where(here, each_slots, slots)

    barrier = pltpu.get_barrier_semaphore()
    greeted = 1
    pl.semaphore_signal(barrier, inc=1, device_id={"vel": partner}, device_id_type=mesh_id)
    for a in range(1, blocks):
        peer = lax.rem(group + a, blocks)
        pl.semaphore_signal(barrier, inc=1, device_id={"epoch": peer}, device_id_type=mesh_id)
        greeted += 1
    if exchange:
        for other in (before, after):
            pl.semaphore_signal(barrier, inc=1, device_id={"sky": other}, device_id_type=mesh_id)
            greeted += 1

    if exchange:
        groups = sent_sides.shape[1]
        lane = lax.broadcasted_iota(jnp.int32, (tile, LANES), 1)

        def side_copy(to_after, g):
            return pltpu.make_async_remote_copy(
                src_ref=sent_sides.at[to_after, g],
                dst_ref=came_sides.at[to_after, g],
                send_sem=sz.at[to_after, g],
                recv_sem=rz.at[to_after, g],
                device_id={"sky": after if to_after else before},
                device_id_type=mesh_id,
            )

        building[...] = jnp.zeros_like(building)

        @pl.when(column == 0)
        def _():
            came_sides[1] = jnp.zeros_like(came_sides[1])

        @pl.when(column == GRID_X - 1)
        def _():
            came_sides[0] = jnp.zeros_like(came_sides[0])

        pl.semaphore_wait(barrier, greeted)

        def weigh(e, carry):
            s = lax.rem(e, slots)
            g = e // slots
            usable = valid[e].astype(jnp.float32)
            inverse = usable / variances[e, 0].astype(jnp.float32)
            scaled = images[e, 0].astype(jnp.float32) * inverse
            to_slot = wide * s
            to_mirror = wide * (slots - 1 - s)
            for m, field in enumerate((scaled, inverse)):
                own[e, m] = field.astype(jnp.bfloat16)
                low = pltpu.roll(field, to_mirror, axis=1)
                high = pltpu.roll(field, lax.rem(to_slot + wide, LANES), axis=1)
                at_low = (lane >= to_mirror) & (lane < to_mirror + wide)
                at_high = (lane >= to_slot) & (lane < to_slot + wide)
                building[0, m] = jnp.where(at_low, low, building[0, m])
                building[1, m] = jnp.where(at_high, high, building[1, m])

            @pl.when((s == slots - 1) | (e == epochs - 1))
            def _():
                sent_sides[0, g] = building[0].astype(jnp.bfloat16)
                sent_sides[1, g] = building[1].astype(jnp.bfloat16)

                @pl.when(column > 0)
                def _():
                    side_copy(0, g).start()

                @pl.when(column < GRID_X - 1)
                def _():
                    side_copy(1, g).start()

            return carry

        lax.fori_loop(0, epochs, weigh, 0)
    else:
        pl.semaphore_wait(barrier, greeted)

    shape = (rows_out, rows_in)
    row_q[...] = exponents(
        positions(lax.broadcasted_iota(jnp.int32, shape, 1), tile)
        - lax.broadcasted_iota(jnp.int32, shape, 0) + REACH
    )
    shape = (LANES, width)
    held = lax.broadcasted_iota(jnp.int32, shape, 0)
    shifted_out = lax.broadcasted_iota(jnp.int32, shape, 1) - REACH
    own_q[...] = exponents(held - shifted_out)
    if exchange:

        def place_strips(s, carry):
            low, high = wide * s, wide * (slots - 1 - s)
            pixel = jnp.where(
                (held >= low) & (held < low + wide),
                held - low - wide,
                jnp.where((held >= high) & (held < high + wide), held - high + tile, 4 * tile),
            )
            side_q[s] = exponents(pixel - shifted_out)
            return carry

        lax.fori_loop(0, slots, place_strips, 0)
    else:
        side_q[0] = exponents(positions(held + tile, tile) - shifted_out)

    first = member * epochs

    at_epoch = lax.broadcasted_iota(jnp.int32, motion.shape[1:], 1)
    moved = jnp.zeros(motion.shape[1:], jnp.int32)
    for way in range(2):
        start = jnp.where(at_epoch == first, motion[way], 0)
        moved += jnp.abs(motion[way] - jnp.sum(start, axis=1, keepdims=True))
    held_here = (at_epoch >= first) & (at_epoch < first + epochs)
    counted = jnp.zeros(ends_made.shape, jnp.int32)
    at_run = lax.broadcasted_iota(jnp.int32, ends_made.shape, 1)
    for run in range(runs - 1):
        count = jnp.sum((held_here & (moved <= run)).astype(jnp.int32), axis=1, keepdims=True)
        counted = jnp.where(at_run == run, count, counted)
    ends_made[...] = counted
    ends_copy = pltpu.make_async_copy(ends_made, ends, ends_sem)
    ends_copy.start()
    plane_a[:maps] = jnp.zeros_like(plane_a[:maps])
    plane_b[:maps] = jnp.zeros_like(plane_b[:maps])

    def correlate(e, turn):
        sigma = jnp.full((8, LANES), sigmas[e], jnp.float32)
        power = 1.0 / (sigma * sigma)
        tap = lax.broadcasted_iota(jnp.int32, (8, LANES), 1) - PSFR
        norm = jnp.sum(jnp.exp(exponents(tap) * power), axis=1, keepdims=True)
        scale = (1.0 / norm)[:1]
        power = power[:1, :1]

        def both(q):
            profile = jnp.exp(q * power) * scale
            return profile.astype(jnp.bfloat16), (profile * profile).astype(jnp.bfloat16)

        row_bands = both(row_q[...])
        s = lax.rem(e, slots) if exchange else 0
        for part, q in enumerate((own_q[...], side_q[s])):
            for m, made in enumerate(both(q)):
                bands[turn, m, part * LANES : (part + 1) * LANES] = made
        if exchange:
            g = e // slots
            lane = lax.broadcasted_iota(jnp.int32, (tile, LANES), 1)
            in_slot = (lane >= wide * s) & (lane < wide * s + wide)
        for m in range(maps):
            if exchange:
                side = jnp.where(
                    in_slot,
                    came_sides[1, g, m].astype(jnp.float32),
                    came_sides[0, g, m].astype(jnp.float32),
                ).astype(jnp.bfloat16)
            else:
                side = halo[e, m]
            held = jnp.concatenate([own[e, m], side], axis=1)
            rows = jnp.dot(row_bands[m], held, preferred_element_type=jnp.float32)
            done = jnp.dot(
                rows.astype(jnp.bfloat16), bands[turn, m], preferred_element_type=jnp.float32
            )
            at = maps * e + m
            plane_a[at + maps] = plane_a[at] + done[:, :LANES]
            plane_b[at + maps] = plane_b[at] + done[:, LANES:]

    step = 2 if epochs % 2 == 0 else 1

    def several(i, carry):
        for turn in range(step):
            correlate(step * i + turn, turn)
        return carry

    if exchange:
        for g in range(groups):

            @pl.when((column < GRID_X - 1) & (g * slots < epochs))
            def _():
                side_copy(0, g).wait_recv()

            @pl.when((column > 0) & (g * slots < epochs))
            def _():
                side_copy(1, g).wait_recv()

            begin = jnp.minimum(g * slots, epochs) // step
            end = jnp.minimum((g + 1) * slots, epochs) // step
            lax.fori_loop(begin, end, several, 0)
    else:
        lax.fori_loop(0, epochs // step, several, 0)

    def vel_copy(at):
        return pltpu.make_async_remote_copy(
            src_ref=send_v.at[at], dst_ref=recv_v.at[at], send_sem=sv.at[at], recv_sem=rv.at[at],
            device_id={"vel": partner}, device_id_type=mesh_id,
        )

    def epoch_copy(at):
        peer = lax.rem(group + 1 + at // block, blocks)
        return pltpu.make_async_remote_copy(
            src_ref=send_x.at[at], dst_ref=recv_x.at[at], send_sem=sx.at[at], recv_sem=rx.at[at],
            device_id={"epoch": peer}, device_id_type=mesh_id,
        )

    def stack(slot, carry):
        a = blocks - 1 - slot // (2 * block)
        turn = lax.rem(slot, 2 * block)
        mine = ((turn > 0) & (lax.rem(turn, 2) == 0)) | (turn == 2 * block - 1)
        b = jnp.where(mine, 0, 1)
        j = jnp.where(turn == 2 * block - 1, block - 1, jnp.where(mine, turn // 2 - 1, (turn + 1) // 2))
        place = a * block + j
        k = (lax.rem(group + a, blocks) * 2 + lax.rem(member + b, 2)) * block + j
        lane = lax.broadcasted_iota(jnp.int32, (tile, LANES), 1)
        summed = [jnp.zeros((tile, LANES), jnp.float32) for _ in range(maps)]
        low = jnp.zeros((), jnp.int32)
        for run in range(runs):
            high = ends[k, run] if run < runs - 1 else epochs
            at = first + jnp.minimum(low, epochs - 1)
            down = offsets[0, k, at] + REACH
            right = offsets[1, k, at] + REACH
            rows = pl.ds(down, tile)
            for m in range(maps):
                left_part = plane_a[maps * high + m, rows, :] - plane_a[maps * low + m, rows, :]
                right_part = plane_b[maps * high + m, rows, :] - plane_b[maps * low + m, rows, :]
                merged = jnp.where(lane >= right, left_part, right_part)
                summed[m] += pltpu.roll(merged, LANES - right, axis=1)
            low = high
        for m in range(maps):
            keep[b, j, m] = summed[m]

        @pl.when(b == 1)
        def _():
            send_v[place] = keep[1, j].astype(jnp.bfloat16)
            vel_copy(place).start()

        @pl.when(b == 0)
        def _():
            vel_copy(place).wait_recv()
            keep[0, j] = keep[0, j] + recv_v[place].astype(jnp.float32)

            @pl.when(a > 0)
            def _():
                send_x[place - block] = keep[0, j].astype(jnp.bfloat16)
                epoch_copy(place - block).start()

        return carry

    ends_copy.wait()
    lax.fori_loop(0, 2 * blocks * block, stack, 0)

    def finish(j, carry):
        total = keep[0, j]
        for a in range(1, blocks):
            at = (a - 1) * block + j
            epoch_copy(at).wait_recv()
            total = total + recv_x[at].astype(jnp.float32)
        psi_out[j] = total[0]
        phi_out[j] = total[1]
        return carry

    lax.fori_loop(0, block, finish, 0)

    def drain_v(at, carry):
        vel_copy(at).wait_send()
        return carry

    lax.fori_loop(0, blocks * block, drain_v, 0)

    def drain_x(at, carry):
        epoch_copy(at).wait_send()
        return carry

    lax.fori_loop(0, (blocks - 1) * block, drain_x, 0)
    if exchange:

        def drain_z(g, carry):
            @pl.when((column > 0) & (g * slots < epochs))
            def _():
                side_copy(0, g).wait_send()

            @pl.when((column < GRID_X - 1) & (g * slots < epochs))
            def _():
                side_copy(1, g).wait_send()

            return carry

        lax.fori_loop(0, groups, drain_z, 0)


def strips(own, tile_count, tile):
    position = (lax.axis_index("sky") + GRID_X // 2) % tile_count
    column = position % GRID_X
    left = shifted(own[..., tile - MARGIN :], "sky", 1)
    right = shifted(own[..., :MARGIN], "sky", -1)
    left = jnp.where(column > 0, left, jnp.zeros_like(left))
    right = jnp.where(column < GRID_X - 1, right, jnp.zeros_like(right))
    blank = jnp.zeros(own.shape[:3] + (LANES - 2 * MARGIN,), jnp.bfloat16)
    both = jnp.concatenate([own, left, right, blank], axis=3)
    upper = shifted(both[:, :, tile - MARGIN :], "sky", GRID_X)
    lower = shifted(both[:, :, :MARGIN], "sky", -GRID_X)
    upper = jnp.where(position >= GRID_X, upper, jnp.zeros_like(upper))
    lower = jnp.where(position < tile_count - GRID_X, lower, jnp.zeros_like(lower))
    blank = jnp.zeros(both.shape[:2] + (LANES - 2 * MARGIN, both.shape[3]), jnp.bfloat16)
    both = jnp.concatenate([both, upper, lower, blank], axis=2)
    return both[..., :tile], both[..., tile:]


def on_device(images, variances, valid, psf_sigma, offsets):
    epochs = images.shape[0]
    tile = images.shape[-1]
    sky = lax.axis_size("sky")
    blocks = lax.axis_size("epoch")
    block = VELS // (blocks * lax.axis_size("vel"))
    exchange = sky == GRID_X
    last_epoch = epochs * blocks * lax.axis_size("vel") - 1
    runs = 1 + 2 * -(-REACH * (epochs - 1) // last_epoch)
    rows_out = -(-(tile + 2 * REACH) // 16) * 16
    devices = blocks * lax.axis_size("vel")
    reaches = [PSFR + -(-REACH * ((at + 1) * epochs - 1) // last_epoch) for at in range(devices)]
    widths = [(wide, LANES // wide // 2 * 2) for wide in reaches]
    slots = max(each for _, each in widths)
    smem = pl.BlockSpec(memory_space=pltpu.SMEM)
    vmem = pl.BlockSpec(memory_space=pltpu.VMEM)
    dma = pltpu.SemaphoreType.DMA
    half = blocks * block
    far = max(1, (blocks - 1) * block)
    scratch = [
        pltpu.VMEM((2 * (epochs + 1), rows_out, LANES), jnp.float32),
        pltpu.VMEM((2 * (epochs + 1), rows_out, LANES), jnp.float32),
        pltpu.SMEM((VELS, LANES), jnp.int32),
        pltpu.VMEM((VELS, LANES), jnp.int32),
        dma(()),
        pltpu.VMEM((rows_out, tile if exchange else tile + LANES), jnp.float32),
        pltpu.VMEM((LANES, 2 * LANES), jnp.float32),
        pltpu.VMEM((slots if exchange else 1, LANES, 2 * LANES), jnp.float32),
        pltpu.VMEM((2, 2, 2 * LANES, 2 * LANES), jnp.bfloat16),
        pltpu.VMEM((half, 2, tile, tile), jnp.bfloat16),
        pltpu.VMEM((half, 2, tile, tile), jnp.bfloat16),
        pltpu.VMEM((far, 2, tile, tile), jnp.bfloat16),
        pltpu.VMEM((far, 2, tile, tile), jnp.bfloat16),
        pltpu.VMEM((2, block, 2, tile, tile), jnp.float32),
        dma((half,)), dma((half,)), dma((far,)), dma((far,)),
    ]
    if exchange:
        groups = -(-epochs // min(each for _, each in widths))
        scratch += [
            pltpu.VMEM((epochs, 2, tile, tile), jnp.bfloat16),
            pltpu.VMEM((2, 2, tile, LANES), jnp.float32),
            pltpu.VMEM((2, groups, 2, tile, LANES), jnp.bfloat16),
            pltpu.VMEM((2, groups, 2, tile, LANES), jnp.bfloat16),
            dma((2, groups)), dma((2, groups)),
        ]
        operands = (offsets, offsets, psf_sigma, valid.reshape(epochs), images, variances)
        in_specs = [smem, vmem, smem, smem, vmem, vmem]
    else:
        usable = valid[:, 0].astype(jnp.float32)[:, None, None]
        inverse = usable / variances[:, 0].astype(jnp.float32)
        scaled = images[:, 0].astype(jnp.float32) * inverse
        own = jnp.stack([scaled.astype(jnp.bfloat16), inverse.astype(jnp.bfloat16)], axis=1)
        operands = (offsets, offsets, psf_sigma) + strips(own, sky, tile)
        in_specs = [smem, vmem, smem, vmem, vmem]
    out = jax.ShapeDtypeStruct((block, tile, tile), jnp.float32)
    psi_sum, phi_sum = pl.pallas_call(
        functools.partial(fused_kernel, (tile, sky, blocks, block, epochs, runs, widths, exchange)),
        out_shape=(out, out),
        in_specs=in_specs,
        out_specs=(vmem, vmem),
        scratch_shapes=scratch,
        compiler_params=pltpu.CompilerParams(
            collective_id=0, has_side_effects=True, vmem_limit_bytes=28 * 2**20
        ),
    )(*operands)
    phi_sum = jnp.maximum(phi_sum, phi_floor)
    likelihood = psi_sum / jnp.sqrt(phi_sum)
    flux = psi_sum / phi_sum
    return (likelihood[:, None], flux[:, None])


def solution(mesh):
    placed = (
        P(("epoch", "vel"), ("field", "sky"), None, None),
        P(("epoch", "vel"), ("field", "sky"), None, None),
        P(("epoch", "vel"), ("field", "sky")),
        P(("field", "epoch", "vel")),
        P(None, None, "epoch"),
    )
    return jax.shard_map(
        on_device,
        mesh=mesh,
        in_specs=placed,
        out_specs=(
            P(("epoch", "vel"), ("field", "sky"), None, None),
            P(("epoch", "vel"), ("field", "sky"), None, None),
        ),
        check_vma=False,
    )
```
